256 devices in a mesh: chan: 8 (over x, core), space: 32 (over z, y).
Axes of the slice: x: 4, y: 4, z: 8, core: 2. Of those that a mesh axis runs over, the one named last changes fastest.
Arguments:
- patches: bfloat16 [32, 64, 512, 256], P('space', None, 'chan'), may hold values from -6 to 6
- patch_weight: bfloat16 [256, 1024], replicated, may hold values from -0.375 to 0.375
- channel_embed: float32 [512, 1024], P('chan'), may hold values from -300 to 300
- score_map: bfloat16 [1024, 16], replicated, may hold values from -0.125 to 0.125
- out_weight: bfloat16 [1024, 1024], replicated, may hold values from -0.1875 to 0.1875
- norm_gain: float32 [1024], replicated, may hold values from 0.25 to 1.75
- up_weight: bfloat16 [1024, 4096], P(None, 'chan'), may hold values from -0.1875 to 0.1875
- down_weight: bfloat16 [4096, 1024], P('chan'), may hold values from -0.09375 to 0.09375
- cotangent: bfloat16 [32, 64, 1024], P('space', 'chan'), may hold values from -4 to 4
Outputs:
- layer_out: bfloat16 [32, 64, 1024], P('space', 'chan')
- up_grad: float32 [1024, 4096], P('space', 'chan')
- down_grad: float32 [4096, 1024], P(('chan', 'space'))
- patch_grad: float32 [256, 1024], P('space', 'chan')
- channel_grad: float32 [512, 1024], P(('chan', 'space'))
The draws below stay inside these ranges and needn't reach their ends.
All inputs are finite; a program needn't handle non-finite values.
Results may differ from the reference program's by a relative error of at most 0.024.
Values may be sent and summed in bfloat16 or wider, within the bound.
No kernel may reach another device: no remote copies, remote signals or barrier semaphores. Data moves between devices by JAX's collectives and lax.ppermute only.
A program may use at most 192 MiB of HBM per device.

```python
import jax
import jax.numpy as jnp
from jax import lax

P_SIZE = 256
D = 1024
HEADS = 16
FF = 4096
CHANNELS = 512
TOK_DEV = 64
STRIPS = 32


def joint_draw(key):
    base = jax.random.fold_in(key, 913)
    map_key, embed_key = jax.random.split(base, 2)
    score = jnp.clip(jax.random.normal(map_key, (D, HEADS), jnp.float32), -4.0, 4.0) / D ** 0.5
    embeds = 0.5 * jnp.clip(jax.random.normal(embed_key, (CHANNELS, D), jnp.float32), -4.0, 4.0)
    return (score, embeds)


def draw_score_map(key, part):
    return joint_draw(key)[0].astype(jnp.bfloat16)


def draw_channel_embed(key, part):
    return joint_draw(key)[1]


def spiked(entries, key, source, target, blocks, factor):
    def block_of(position):
        return (jnp.arange(entries.shape[position]) // (entries.shape[position] // blocks)).reshape((-1,) + (1,) * (entries.ndim - 1 - position))

    first = jax.random.permutation(key, blocks)[block_of(target)]
    far = (block_of(target) + blocks // 2) % blocks
    return jnp.where((block_of(source) == first) | (block_of(source) == far), factor * entries, entries)


def level_of(key, extent, shards, low, largest):
    gain = 1.0
    for dim, parts in shards:
        heights = jax.random.uniform(jax.random.fold_in(jax.random.fold_in(key, 6), dim), (parts,), jnp.float32, low / len(shards), largest / len(shards))
        gain = gain * jnp.repeat(jnp.exp(heights), extent[dim] // parts).reshape((-1,) + (1,) * (len(extent) - 1 - dim))
    return gain


def bell_draw(stream_key, shape, spread, bound, shards=(), dtype=jnp.bfloat16):
    level = level_of(stream_key, shape, shards, -0.22, 0.18) if shards else 1.0
    array = jax.random.normal(stream_key, shape, jnp.float32) * spread * level
    return jnp.minimum(jnp.maximum(array, -bound), bound).astype(dtype)


def gaussian_with(key, extent, spread, reach, pieces, heavy, dtype=jnp.bfloat16):
    entries = spread * jax.random.normal(key, extent, jnp.float32)
    if pieces:
        entries = entries * level_of(key, extent, pieces, -0.22, 0.18)
    return jnp.clip(spiked(entries, jax.random.fold_in(key, 3), *heavy), -reach, reach).astype(dtype)


def setup_inputs(seed: int = 0) -> dict:
    arg_keys = jax.random.split(jax.random.key(seed), 10)
    patches = gaussian_with(arg_keys[0], (STRIPS, TOK_DEV, CHANNELS, P_SIZE), 1.0, 6.0, ((0, 32), (2, 8)), (0, 3, 32, 2.75))
    patch_weight = bell_draw(arg_keys[1], (P_SIZE, D), P_SIZE ** -0.5, 0.375)
    channel_embed = draw_channel_embed(jax.random.fold_in(arg_keys[9], 71), 0)
    score_map = draw_score_map(jax.random.fold_in(arg_keys[9], 71), 0)
    out_weight = bell_draw(arg_keys[4], (D, D), D ** -0.5, 0.1875)
    norm_gain = jnp.clip(1.0 + 0.15 * jax.random.normal(arg_keys[5], (D,), jnp.float32), 0.25, 1.75)
    up_weight = bell_draw(arg_keys[6], (D, FF), D ** -0.5, 0.1875, ((1, 8),))
    down_weight = bell_draw(arg_keys[7], (FF, D), FF ** -0.5, 0.09375, ((0, 8),))
    cotangent = bell_draw(arg_keys[8], (STRIPS, TOK_DEV, D), 0.25, 4.0, ((0, 32), (1, 8)))
    return {"patches": patches, "patch_weight": patch_weight, "channel_embed": channel_embed, "score_map": score_map, "out_weight": out_weight, "norm_gain": norm_gain, "up_weight": up_weight, "down_weight": down_weight, "cotangent": cotangent}


EPSILON = 1e-06

def root_norm(values, norm_gain):
    return values * lax.rsqrt(lax.optimization_barrier(jnp.mean(values * values, axis=-1, keepdims=True)) + EPSILON) * norm_gain

def reference(patches, patch_weight, channel_embed, score_map, out_weight, norm_gain, up_weight, down_weight, cotangent):
    tokens = patches.shape[1]
    channels = patches.shape[2]
    pixels = patches.shape[3]
    model_width = patch_weight.shape[1]
    head_count = score_map.shape[1]
    head_size = model_width // head_count

    def one_strip(carry, items):
        strip_patches, strip_grad = items
        flat_pixels = strip_patches.reshape(tokens * channels, pixels)
        embedded = lax.optimization_barrier((jnp.dot(flat_pixels, patch_weight, preferred_element_type=jnp.float32).reshape(tokens, channels, model_width) + channel_embed[None]).astype(jnp.bfloat16))
        embed_heads = embedded.reshape(tokens, channels, head_count, head_size).astype(jnp.float32)
        scores = jnp.dot(embedded.reshape(tokens * channels, model_width), score_map, preferred_element_type=jnp.float32).reshape(tokens, channels, head_count)
        highest = lax.optimization_barrier(jnp.max(scores, axis=1, keepdims=True))
        weights = jnp.exp(scores - highest)
        probs = weights / lax.optimization_barrier(jnp.sum(weights, axis=1, keepdims=True))
        weighted = jnp.einsum('tch,tchk->thk', probs, embed_heads, precision=lax.Precision.HIGHEST)
        aggregate = lax.optimization_barrier(weighted.reshape(tokens, model_width).astype(jnp.bfloat16))
        mixing = jnp.dot(aggregate, out_weight, preferred_element_type=jnp.float32)
        normed_full, norm_pull = jax.vjp(lambda values: root_norm(values, norm_gain), mixing)
        normed = normed_full.astype(jnp.bfloat16)
        hidden_pre = jnp.dot(normed, up_weight, preferred_element_type=jnp.float32)
        activated_full, gelu_pull = jax.vjp(jax.nn.gelu, hidden_pre)
        activated = activated_full.astype(jnp.bfloat16)
        layer_rows = (mixing + jnp.dot(activated, down_weight, preferred_element_type=jnp.float32)).astype(jnp.bfloat16)
        grad_act = jnp.dot(strip_grad, down_weight.T, preferred_element_type=jnp.float32)
        grad_pre = gelu_pull(grad_act)[0].astype(jnp.bfloat16)
        down_term = jnp.dot(activated.T, strip_grad, preferred_element_type=jnp.float32)
        up_term = jnp.dot(normed.T, grad_pre, preferred_element_type=jnp.float32)
        grad_norm = jnp.dot(grad_pre, up_weight.T, preferred_element_type=jnp.float32)
        grad_mix = strip_grad.astype(jnp.float32) + norm_pull(grad_norm)[0]
        grad_agg = jnp.dot(grad_mix.astype(jnp.bfloat16), out_weight.T, preferred_element_type=jnp.float32)
        grad_split = grad_agg.reshape(tokens, head_count, head_size)
        agg_dot = lax.optimization_barrier(jnp.sum(grad_split * aggregate.astype(jnp.float32).reshape(tokens, head_count, head_size), axis=-1))
        head_dots = jnp.einsum('thk,tchk->tch', grad_split, embed_heads, precision=lax.Precision.HIGHEST)
        score_grad = (probs * (head_dots - agg_dot[:, None, :])).astype(jnp.bfloat16)
        through_scores = jnp.dot(score_grad.reshape(tokens * channels, head_count), score_map.T, preferred_element_type=jnp.float32)
        grad_embed = lax.optimization_barrier(((probs[..., None] * grad_split[:, None]).reshape(tokens, channels, model_width) + through_scores.reshape(tokens, channels, model_width)).astype(jnp.bfloat16))
        patch_term = jnp.dot(flat_pixels.T, grad_embed.reshape(tokens * channels, model_width), preferred_element_type=jnp.float32)
        channel_term = lax.optimization_barrier(jnp.sum(grad_embed.astype(jnp.float32), axis=0))
        carry = (carry[0] + up_term, carry[1] + down_term, carry[2] + patch_term, carry[3] + channel_term)
        return (carry, layer_rows)
    start_carry = (jnp.zeros(up_weight.shape, jnp.float32), jnp.zeros(down_weight.shape, jnp.float32), jnp.zeros(patch_weight.shape, jnp.float32), jnp.zeros(channel_embed.shape, jnp.float32))
    totals, layer_out = lax.scan(one_strip, start_carry, (patches, cotangent))
    return (layer_out, totals[0], totals[1], totals[2], totals[3])
```

```python
import functools

import jax
import jax.numpy as jnp
import numpy as np
from jax import lax
from jax.experimental import pallas as pl
from jax.experimental.pallas import tpu as pltpu
from jax.sharding import Mesh
from jax.sharding import PartitionSpec as P

EPSILON = 1e-06
F32, BF16 = jnp.float32, jnp.bfloat16
TOK, CH, PIX, D, HEADS, HS = 64, 64, 256, 1024, 16, 64
FFL = 512
PAY = D + 128
GROUP = 4
CHAN, SPACE = ("x", "core"), ("z", "y")
NCHAN, NSPACE, NY, NZ = 8, 32, 4, 8


def dot(a, b):
    return lax.dot_general(a, b, (((1,), (0,)), ((), ())), preferred_element_type=F32)


def dot_nt(a, b):
    return lax.dot_general(a, b, (((1,), (1,)), ((), ())), preferred_element_type=F32)


def dot_tn(a, b):
    return lax.dot_general(a, b, (((0,), (0,)), ((), ())), preferred_element_type=F32)


def iota(shape, dim):
    return lax.broadcasted_iota(jnp.int32, shape, dim)


def split2(x):
    hi = x.astype(BF16)
    return hi, (x - hi.astype(F32)).astype(BF16)


def split3(x):
    hi = x.astype(BF16)
    rest = x - hi.astype(F32)
    mid = rest.astype(BF16)
    low = (rest - mid.astype(F32)).astype(BF16)
    return hi, mid, low


def transposed_map(s):
    eye = (iota((HEADS, HEADS), 0) == iota((HEADS, HEADS), 1)).astype(F32).astype(BF16)
    return dot_nt(eye, s).astype(BF16)


def head_select(rows):
    shape = (rows, HEADS, D)
    return iota(shape, 2) // HS == iota(shape, 1)


def head_spread():
    shape = (128, D)
    return (iota(shape, 1) // HS == iota(shape, 0)).astype(F32).astype(BF16)


def pack_parts(x):
    lane = iota(x.shape, 1)
    x = jnp.where(lane < HEADS, x, 0.0)
    hi, mid, low = (v.astype(F32) for v in split3(x))
    return (hi + pltpu.roll(mid, HEADS, 1) + pltpu.roll(low, 2 * HEADS, 1)).astype(BF16)


def unpack_parts(x):
    x = x.astype(F32)
    whole = x + pltpu.roll(x, 128 - HEADS, 1) + pltpu.roll(x, 128 - 2 * HEADS, 1)
    return jnp.where(iota(x.shape, 1) < HEADS, whole, 0.0)


def as_column(x, rows):
    shape = (rows, HEADS, 128)
    mask = iota(shape, 2) == iota(shape, 1)
    picked = jnp.where(mask, jnp.broadcast_to(x[:, None, :], shape), 0.0)
    return jnp.sum(picked, axis=2, keepdims=True).reshape(rows * HEADS, 1)


def as_lanes(col, rows):
    shape = (rows, HEADS, 128)
    mask = iota(shape, 2) == iota(shape, 1)
    full = jnp.broadcast_to(col, (rows * HEADS, 128)).reshape(shape)
    return jnp.sum(jnp.where(mask, full, 0.0), axis=1)


def same_token():
    shape = (GROUP * HEADS, GROUP * CH)
    return iota(shape, 0) // HEADS == iota(shape, 1) // CH


def forward_kernel(x_ref, w_ref, s_ref, e_ref, score_ref, pay_ref, e4_ref):
    st = transposed_map(s_ref[...])
    w2 = jnp.concatenate(split2(dot_nt(st, w_ref[...])), axis=0)
    e_hi, e_low = split2(e_ref[...])
    es = dot_nt(st, e_hi) + dot_nt(st, e_low)
    es4 = jnp.concatenate([es] * GROUP, axis=1)
    for k in range(GROUP):
        e4_ref[k * CH : (k + 1) * CH, :] = e_hi
    block = GROUP * CH

    @pl.loop(0, TOK // 8)
    def _(it):
        outs, cols = [], []
        for half in range(2):
            at = pl.multiple_of(it * 2 * block + half * block, block)
            xg = x_ref[pl.ds(at, block), :]
            s2 = dot_nt(w2, xg)
            s = s2[:HEADS] + s2[HEADS:] + es4
            score_ref[:, pl.ds(at, block)] = s
            mask = same_token()
            sx = jnp.where(mask, jnp.concatenate([s] * GROUP, axis=0), -jnp.inf)
            m = jnp.max(sx, axis=1, keepdims=True)
            w = jnp.exp(sx - m)
            total = jnp.sum(w, axis=1, keepdims=True)
            wb = w.astype(BF16)
            y = dot(wb, xg).astype(BF16)
            out = dot(y, w_ref[...]) + dot(wb, e4_ref[...])
            outs.append(out * (1.0 / total))
            cols.append(m + jnp.log(total))
        out = jnp.concatenate(outs, axis=0).reshape(8, HEADS, D)
        out = jnp.sum(jnp.where(head_select(8), out, 0.0), axis=1)
        rows = pl.ds(pl.multiple_of(it * 8, 8), 8)
        pay_ref[rows, :D] = out.astype(BF16)
        pay_ref[rows, D:] = pack_parts(as_lanes(jnp.concatenate(cols, axis=0), 8))


def combine_kernel(part_ref, ow_ref, gain_ref, pay_ref, agg_ref, mix_ref):
    lse = unpack_parts(part_ref[:, :, D:].reshape(NCHAN * 8, 128)).reshape(NCHAN, 8, 128)
    top = jnp.max(lse, axis=0, keepdims=True)
    e = jnp.exp(lse - top)
    total = jnp.sum(e, axis=0, keepdims=True)
    whole = (top + jnp.log(total))[0]
    weight = (e / total).reshape(NCHAN * 8, 128)
    hi, low = split2(weight)
    spread = head_spread()
    wide = (dot(hi, spread) + dot(low, spread)).reshape(NCHAN, 8, D)
    agg = jnp.sum(part_ref[:, :, :D].astype(F32) * wide, axis=0).astype(BF16)
    mix = dot(agg, ow_ref[...])
    scale = lax.rsqrt(jnp.mean(mix * mix, axis=1, keepdims=True) + EPSILON)
    normed = (mix * scale * gain_ref[...]).astype(BF16)
    parts = pack_parts(whole)
    for j in range(NCHAN):
        pay_ref[j, :, :D] = normed
        pay_ref[j, :, D:] = parts
    agg_ref[...] = agg
    mix_ref[...] = mix


def mlp_kernel(n_ref, up_ref, down_ref, cot_ref, act_ref, gpre_ref, gn_ref):
    normed = n_ref[:, :, :D].reshape(TOK, D)
    cot = cot_ref[...].reshape(TOK, D)
    x = dot(normed, up_ref[...])
    c = np.float32(np.sqrt(2 / np.pi))
    t = jnp.tanh(c * (x + 0.044715 * (x * x * x)))
    act_ref[...] = (0.5 * x * (1.0 + t)).astype(BF16)
    slope = 0.5 * (1.0 + t) + 0.5 * x * (1.0 - t * t) * (c * (1.0 + (3 * 0.044715) * (x * x)))
    gpre = (dot_nt(cot, down_ref[...]) * slope).astype(BF16)
    gpre_ref[...] = gpre
    gn_ref[...] = dot_nt(gpre, up_ref[...]).astype(BF16).reshape(NCHAN, 8, D)


def mlp_out_kernel(n_ref, act_ref, gpre_ref, down_ref, out_ref, ypay_ref):
    act = act_ref[...]
    out_ref[...] = dot(act, down_ref[...]).astype(BF16).reshape(NCHAN, 8, D)
    source, target = iota((FFL, FFL), 0), iota((FFL, FFL), 1)
    y, rest = target // 128, target % 128
    perm = (source == (rest // 16) * 64 + y * 16 + rest % 16).astype(F32).astype(BF16)
    act_y = dot(act, perm).astype(BF16)
    normed = n_ref[:, :, :D].reshape(TOK, D)
    gpre = gpre_ref[...]
    source, target = iota((D, D), 0), iota((D, D), 1)
    y, rest = target // 256, target % 256
    perm = (source == (rest // 32) * 128 + y * 32 + rest % 32).astype(F32).astype(BF16)
    norm_y = dot(normed, perm).astype(BF16)
    for k in range(NY):
        ypay_ref[k, :, :FFL] = gpre
        ypay_ref[k, :, FFL : FFL + 128] = act_y[:, 128 * k : 128 * (k + 1)]
        ypay_ref[k, :, FFL + 128 :] = norm_y[:, 256 * k : 256 * (k + 1)]


def weight_kernel(in_ref, cot_ref, out_ref):
    rows = NY * TOK
    gpre = in_ref[:, :, :FFL].reshape(rows, FFL)
    act = in_ref[:, :, FFL : FFL + 128].reshape(rows, 128)
    normed = in_ref[:, :, FFL + 128 :].reshape(rows, 256)
    cot = cot_ref[...].reshape(rows, D)
    out_ref[:, :32, :] = dot_tn(normed, gpre).astype(BF16).reshape(NZ, 32, FFL)
    down = dot_tn(act, cot).astype(BF16)
    out_ref[:, 32:48, :] = down[:, :FFL].reshape(NZ, 16, FFL)
    out_ref[:, 48:, :] = down[:, FFL:].reshape(NZ, 16, FFL)


def mix_grad_kernel(gn_ref, mix_ref, agg_ref, cot_ref, ow_ref, gain_ref, pay_ref):
    gn = jnp.sum(gn_ref[...].astype(F32), axis=0)
    mix = mix_ref[...]
    scale = lax.rsqrt(jnp.mean(mix * mix, axis=1, keepdims=True) + EPSILON)
    g = gn * gain_ref[...]
    pull = g * scale - mix * (scale * scale * scale * jnp.mean(mix * g, axis=1, keepdims=True))
    half = (cot_ref[...].astype(F32) + pull).astype(BF16)
    ga = dot_nt(half, ow_ref[...]).astype(BF16)
    hi, mid, low = split3(ga.astype(F32) * agg_ref[...].astype(F32))
    spread = head_spread()
    dots = dot_nt(hi, spread) + dot_nt(mid, spread) + dot_nt(low, spread)
    parts = pack_parts(dots)
    for j in range(NCHAN):
        pay_ref[j, :, :D] = ga
        pay_ref[j, :, D:] = parts


def backward_kernel(
    x_ref, w_ref, s_ref, e_ref, score_ref, lse_ref, ga_ref, patch_ref, chan_ref,
    e4_ref, left_ref, right_ref, z_ref, sg_ref,
):
    st = transposed_map(s_ref[...])
    e_hi = e_ref[...].astype(BF16)
    for k in range(GROUP):
        e4_ref[k * CH : (k + 1) * CH, :] = e_hi
    block = GROUP * CH
    z_ref[...] = jnp.zeros_like(z_ref)
    sg_ref[...] = jnp.zeros_like(sg_ref)

    @pl.loop(0, TOK // 8)
    def _(it):
        ga = ga_ref[it, :, :D].astype(F32)
        gx = jnp.where(head_select(8), jnp.broadcast_to(ga[:, None, :], (8, HEADS, D)), 0.0)
        gx = gx.reshape(8 * HEADS, D).astype(BF16)
        here = pl.ds(pl.multiple_of(it * 8 * HEADS, 8 * HEADS), 8 * HEADS)
        right_ref[here, :] = gx
        dots = as_column(unpack_parts(ga_ref[it, :, D:]), 8)
        lse = as_column(unpack_parts(lse_ref[it, :, D:]), 8)
        back = dot_nt(gx, w_ref[...]).astype(BF16)
        back_e = dot_nt(gx, e4_ref[...])
        for half in range(2):
            at = pl.multiple_of(it * 2 * block + half * block, block)
            rows = slice(half * GROUP * HEADS, (half + 1) * GROUP * HEADS)
            xg = x_ref[pl.ds(at, block), :]
            s = score_ref[:, pl.ds(at, block)]
            mask = same_token()
            sx = jnp.where(mask, jnp.concatenate([s] * GROUP, axis=0) - lse[rows], -jnp.inf)
            p = jnp.exp(sx)
            head_dots = dot_nt(back[rows], xg) + back_e[rows]
            sg = p * (head_dots - dots[rows])
            sg = jnp.sum(sg.reshape(GROUP, HEADS, block), axis=0)
            both = jnp.concatenate([p, sg], axis=0).astype(BF16)
            yz = dot(both, xg)
            base = pl.multiple_of(it * 8 * HEADS + half * GROUP * HEADS, GROUP * HEADS)
            left_ref[pl.ds(base, GROUP * HEADS), :PIX] = yz[: GROUP * HEADS].astype(BF16)
            z_ref[...] += yz[GROUP * HEADS :]
            sg_ref[...] += sg
            pc = p[:, :CH] + p[:, CH : 2 * CH] + p[:, 2 * CH : 3 * CH] + p[:, 3 * CH :]
            left_ref[pl.ds(base, GROUP * HEADS), PIX:] = jnp.concatenate([pc, pc], axis=1).astype(BF16)

    sg = sg_ref[...]
    sgc = sg[:, :CH] + sg[:, CH : 2 * CH] + sg[:, 2 * CH : 3 * CH] + sg[:, 3 * CH :]
    last = jnp.concatenate([z_ref[...], sgc, sgc], axis=1)
    tail_hi, tail_low = split2(last)
    out = dot_tn(left_ref[...], right_ref[...]) + dot_tn(tail_hi, st) + dot_tn(tail_low, st)
    for j in range(NCHAN):
        patch_ref[j] = out[:PIX, 128 * j : 128 * (j + 1)].astype(BF16)
    chan_ref[...] = out[PIX : PIX + CH, :].astype(BF16)


def call(kernel, outs, scratch=(), flops=0, nbytes=0, **kw):
    return pl.pallas_call(
        kernel,
        out_shape=[jax.ShapeDtypeStruct(s, d) for s, d in outs],
        scratch_shapes=list(scratch),
        cost_estimate=pl.CostEstimate(flops=flops, bytes_accessed=nbytes, transcendentals=0),
        compiler_params=pltpu.CompilerParams(vmem_limit_bytes=48 << 20),
        **kw,
    )


def exchange(x, axes):
    return lax.all_to_all(x, axes, 0, 0, tiled=True)


def to_all(x, axes, n):
    return exchange(jnp.broadcast_to(x[None], (n,) + x.shape), axes)


def on_device(
    patches, patch_weight, channel_embed, score_map, out_weight, norm_gain, up_weight, down_weight, cotangent
):
    x = patches.reshape(TOK * CH, PIX)
    gain = norm_gain.reshape(1, D)
    own_cot = cotangent[0]
    cot = to_all(own_cot, CHAN, NCHAN)
    cot4 = to_all(cot.reshape(TOK, D), ("y",), NY).reshape(NY, TOK, D)

    score, pay = call(
        forward_kernel,
        [((HEADS, TOK * CH), F32), ((TOK, PAY), BF16)],
        [pltpu.VMEM((GROUP * CH, D), BF16)],
        flops=20 << 30, nbytes=4 << 20,
    )(x, patch_weight, score_map, channel_embed)
    parts = exchange(pay.reshape(NCHAN, 8, PAY), CHAN)
    npay, agg, mix = call(
        combine_kernel,
        [((NCHAN, 8, PAY), BF16), ((8, D), BF16), ((8, D), F32)],
        flops=1 << 30, nbytes=3 << 20,
    )(parts, out_weight, gain)
    nfull = exchange(npay, CHAN)
    act, gpre, gn = call(
        mlp_kernel,
        [((TOK, FFL), BF16), ((TOK, FFL), BF16), ((NCHAN, 8, D), BF16)],
        flops=1 << 30, nbytes=3 << 20,
    )(nfull, up_weight, down_weight, cot)
    gn_parts = exchange(gn, CHAN)
    out_part, ypay = call(
        mlp_out_kernel,
        [((NCHAN, 8, D), BF16), ((NY, TOK, 896), BF16)],
        flops=1 << 30, nbytes=3 << 20,
    )(nfull, act, gpre, down_weight)
    out_parts = exchange(out_part, CHAN)
    yfull = exchange(ypay, ("y",))
    (gpay,) = call(
        mix_grad_kernel, [((NCHAN, 8, PAY), BF16)], flops=1 << 30, nbytes=3 << 20
    )(gn_parts, mix, agg, own_cot, out_weight, gain)
    gfull = exchange(gpay, CHAN)
    (zpay,) = call(
        weight_kernel, [((NZ, 64, FFL), BF16)], flops=1 << 30, nbytes=3 << 20
    )(yfull, cot4)
    zfull = exchange(zpay, ("z",))
    patch, chan = call(
        backward_kernel,
        [((NCHAN, PIX, 128), BF16), ((CH, D), BF16)],
        [
            pltpu.VMEM((GROUP * CH, D), BF16),
            pltpu.VMEM((TOK * HEADS, PIX + 128), BF16),
            pltpu.VMEM((TOK * HEADS, D), BF16),
            pltpu.VMEM((HEADS, PIX), F32),
            pltpu.VMEM((HEADS, GROUP * CH), F32),
        ],
        flops=20 << 30, nbytes=6 << 20,
    )(x, patch_weight, score_map, channel_embed, score, nfull, gfull)
    patch = jnp.sum(exchange(patch, CHAN).astype(F32), axis=0).astype(BF16)
    last = jnp.concatenate(
        [patch.reshape(NSPACE, 1, D), chan.reshape(NSPACE, 2, D)], axis=1
    )
    last = jnp.sum(exchange(last, SPACE).astype(F32), axis=0)
    layer_out = (mix + jnp.sum(out_parts.astype(F32), axis=0)).astype(BF16)[None]
    weights = jnp.sum(zfull.astype(F32), axis=0)
    up_grad = weights[:32]
    down_grad = jnp.concatenate([weights[32:48], weights[48:]], axis=1)
    return layer_out, up_grad, down_grad, last[0].reshape(8, 128), last[1:]


def solution(mesh):
    fine = Mesh(np.asarray(mesh.devices).reshape(4, 2, NZ, NY), ("x", "core", "z", "y"))
    return jax.shard_map(
        on_device,
        mesh=fine,
        in_specs=(
            P(SPACE, None, CHAN, None),
            P(),
            P(CHAN, None),
            P(),
            P(),
            P(),
            P(None, CHAN),
            P(CHAN, None),
            P(SPACE, CHAN, None),
        ),
        out_specs=(
            P(SPACE, CHAN, None),
            P(SPACE, CHAN),
            P((*CHAN, *SPACE), None),
            P(SPACE, CHAN),
            P((*CHAN, *SPACE), None),
        ),
        check_vma=False,
    )
```

```python
import functools

import jax
import jax.numpy as jnp
import numpy as np
from jax import lax
from jax.experimental import pallas as pl
from jax.experimental.pallas import tpu as pltpu
from jax.sharding import Mesh
from jax.sharding import PartitionSpec as P

EPSILON = 1e-06
F32, BF16 = jnp.float32, jnp.bfloat16
TOK, CH, PIX, D, HEADS, HS = 64, 64, 256, 1024, 16, 64
FFL = 512
PAY = D + 128
GROUP = 4
CHAN, SPACE = ("x", "core"), ("z", "y")
NCHAN, NSPACE, NX, NY, NZ = 8, 32, 4, 4, 8
HALF = TOK // 2


def dot(a, b):
    return lax.dot_general(a, b, (((1,), (0,)), ((), ())), preferred_element_type=F32)


def dot_nt(a, b):
    return lax.dot_general(a, b, (((1,), (1,)), ((), ())), preferred_element_type=F32)


def dot_tn(a, b):
    return lax.dot_general(a, b, (((0,), (0,)), ((), ())), preferred_element_type=F32)


def iota(shape, dim):
    return lax.broadcasted_iota(jnp.int32, shape, dim)


def split2(x):
    hi = x.astype(BF16)
    return hi, (x - hi.astype(F32)).astype(BF16)


def split3(x):
    hi = x.astype(BF16)
    rest = x - hi.astype(F32)
    mid = rest.astype(BF16)
    low = (rest - mid.astype(F32)).astype(BF16)
    return hi, mid, low


def head_select(rows):
    shape = (rows, HEADS, D)
    return iota(shape, 2) // HS == iota(shape, 1)


def head_spread():
    shape = (128, D)
    return (iota(shape, 1) // HS == iota(shape, 0)).astype(F32).astype(BF16)


def pack_parts(x):
    lane = iota(x.shape, 1)
    x = jnp.where(lane < HEADS, x, 0.0)
    hi, mid, low = (v.astype(F32) for v in split3(x))
    return (hi + pltpu.roll(mid, HEADS, 1) + pltpu.roll(low, 2 * HEADS, 1)).astype(BF16)


def unpack_parts(x):
    x = x.astype(F32)
    whole = x + pltpu.roll(x, 128 - HEADS, 1) + pltpu.roll(x, 128 - 2 * HEADS, 1)
    return jnp.where(iota(x.shape, 1) < HEADS, whole, 0.0)


def as_column(x, rows):
    shape = (rows, HEADS, 128)
    mask = iota(shape, 2) == iota(shape, 1)
    picked = jnp.where(mask, jnp.broadcast_to(x[:, None, :], shape), 0.0)
    return jnp.sum(picked, axis=2, keepdims=True).reshape(rows * HEADS, 1)


def as_lanes(col, rows):
    shape = (rows, HEADS, 128)
    mask = iota(shape, 2) == iota(shape, 1)
    full = jnp.broadcast_to(col, (rows * HEADS, 128)).reshape(shape)
    return jnp.sum(jnp.where(mask, full, 0.0), axis=1)


def fold(x):
    return x[:, :CH] + x[:, CH : 2 * CH] + x[:, 2 * CH : 3 * CH] + x[:, 3 * CH :]


def same_token():
    shape = (GROUP * HEADS, GROUP * CH)
    return iota(shape, 0) // HEADS == iota(shape, 1) // CH


def chunks(src, dst, sems, first):
    size = 8 * CH

    def chunk(k):
        rows = pl.ds(pl.multiple_of(k * size, size), size)
        return pltpu.make_async_copy(src.at[rows, :], dst.at[rows, :], sems.at[first + k])

    return chunk


def forward_kernel(
    x_hbm, w_hbm, st_hbm, e_hbm, score_ref, keep_ref, send_ref, w_ref, st_ref, eh_ref,
    x_ref, e_ref, y_ref, p_ref, lane_ref, sems,
):
    loads = [
        pltpu.make_async_copy(src, dst, sems.at[k])
        for k, (src, dst) in enumerate(((st_hbm, st_ref), (w_hbm, w_ref), (e_hbm, e_ref)))
    ]
    for copy in loads:
        copy.start()
    block = GROUP * CH
    octet = 2 * block
    chunk = chunks(x_hbm, x_ref, sems, 3)
    for k in range(TOK // 8):
        chunk(k).start()
    for copy in loads:
        copy.wait()
    st = st_ref[...]
    w2 = jnp.concatenate(split2(dot_nt(st, w_ref[...])), axis=0)
    e_hi, e_low = split2(e_ref[...])
    eh_ref[...] = e_hi
    es = dot_nt(st, e_hi) + dot_nt(st, e_low)
    es4 = jnp.concatenate([es] * GROUP, axis=1)
    core = lax.axis_index("core")

    @pl.loop(0, TOK // 8)
    def _(it):
        chunk(it).wait()
        cols = []
        for half in range(2):
            at = pl.multiple_of(it * octet + half * block, block)
            xg = x_ref[pl.ds(at, block), :]
            s2 = dot_nt(w2, xg)
            s = s2[:HEADS] + s2[HEADS:] + es4
            score_ref[:, pl.ds(at, block)] = s
            sx = jnp.where(same_token(), jnp.concatenate([s] * GROUP, axis=0), -jnp.inf)
            m = jnp.max(sx, axis=1, keepdims=True)
            w = jnp.exp(sx - m)
            total = jnp.sum(w, axis=1, keepdims=True)
            w = w * (1.0 / total)
            rows = pl.ds(pl.multiple_of((2 * it + half) * GROUP * HEADS, GROUP * HEADS), GROUP * HEADS)
            y_ref[rows, :] = dot(w.astype(BF16), xg).astype(BF16)
            p_ref[rows, :] = fold(w).astype(BF16)
            cols.append(m + jnp.log(total))
        lane_ref[pl.ds(pl.multiple_of(it * 8, 8), 8), :] = as_lanes(jnp.concatenate(cols, axis=0), 8)

    @pl.loop(0, TOK // 16)
    def _(it):
        rows = pl.ds(pl.multiple_of(it * 16 * HEADS, 16 * HEADS), 16 * HEADS)
        out = dot(y_ref[rows, :], w_ref[...]) + dot(p_ref[rows, :], eh_ref[...])
        out = jnp.where(head_select(16), out.reshape(16, HEADS, D), 0.0)
        out = jnp.sum(out, axis=1)
        parts = lane_ref[pl.ds(pl.multiple_of(it * 16, 16), 16), :]
        first = core == 0
        to = pl.ds(pl.multiple_of(it * 8, 8), 8)
        keep_ref[to, :D] = jnp.where(first, out[:8], out[8:]).astype(BF16)
        send_ref[to, :D] = jnp.where(first, out[8:], out[:8]).astype(BF16)
        keep_ref[to, D:] = pack_parts(jnp.where(first, parts[:8], parts[8:]))
        send_ref[to, D:] = pack_parts(jnp.where(first, parts[8:], parts[:8]))


def merge(outs, parts):
    rows = outs[0].shape[0]
    lses = [unpack_parts(p) for p in parts]
    top = functools.reduce(jnp.maximum, lses)
    es = [jnp.exp(v - top) for v in lses]
    total = sum(es)
    weight = jnp.concatenate([e / total for e in es], axis=0)
    hi, low = split2(weight)
    spread = head_spread()
    wide = dot(hi, spread) + dot(low, spread)
    out = sum(o.astype(F32) * wide[k * rows : (k + 1) * rows] for k, o in enumerate(outs))
    return out, top + jnp.log(total)


def pair_kernel(keep_ref, got_ref, cot_ref, pay_ref):
    out, lse = merge([keep_ref[:, :D], got_ref[:, :D]], [keep_ref[:, D:], got_ref[:, D:]])
    pay_ref[:HALF, :D] = out.astype(BF16)
    pay_ref[:HALF, D:] = pack_parts(lse)
    pay_ref[HALF:, :D] = cot_ref[...]
    pay_ref[HALF:, D:] = jnp.zeros((8, 128), BF16)


def combine_kernel(p0_ref, p1_ref, p2_ref, p3_ref, ow_ref, gain_ref, pay_ref, agg_ref, mix_ref):
    refs = (p0_ref, p1_ref, p2_ref, p3_ref)
    out, lse = merge([r[:HALF, :D] for r in refs], [r[:HALF, D:] for r in refs])
    agg = out.astype(BF16)
    mix = dot(agg, ow_ref[...])
    scale = lax.rsqrt(jnp.mean(mix * mix, axis=1, keepdims=True) + EPSILON)
    pay_ref[:, :D] = (mix * scale * gain_ref[...]).astype(BF16)
    pay_ref[:, D:PAY] = pack_parts(lse)
    x = lax.axis_index("x")
    for k in range(NX):
        rows = pl.ds(pl.multiple_of(lax.rem(x + (NX - k), NX) * 8, 8), 8)
        pay_ref[rows, PAY:] = refs[k][HALF:, :D]
    agg_ref[...] = agg
    mix_ref[...] = mix


def tokens(a_ref, b_ref, start, stop):
    return jnp.concatenate([a_ref[:, start:stop], b_ref[:, start:stop]], axis=0)


def mlp_kernel(a_ref, b_ref, up_ref, down_ref, act_ref, gpre_ref, keep_ref, send_ref):
    normed = tokens(a_ref, b_ref, 0, D)
    cot = tokens(a_ref, b_ref, PAY, PAY + D)
    x = dot(normed, up_ref[...])
    c = np.float32(np.sqrt(2 / np.pi))
    t = jnp.tanh(c * (x + 0.044715 * (x * x * x)))
    act_ref[...] = (0.5 * x * (1.0 + t)).astype(BF16)
    slope = 0.5 * (1.0 + t) + 0.5 * x * (1.0 - t * t) * (c * (1.0 + (3 * 0.044715) * (x * x)))
    gpre = (dot_nt(cot, down_ref[...]) * slope).astype(BF16)
    gpre_ref[...] = gpre
    gn = dot_nt(gpre, up_ref[...]).astype(BF16)
    keep_ref[...] = gn[:HALF]
    send_ref[...] = gn[HALF:]


def mlp_out_kernel(a_ref, b_ref, act_ref, gpre_ref, down_ref, keep_ref, send_ref, ypay_ref):
    act = act_ref[...]
    out = dot(act, down_ref[...]).astype(BF16)
    keep_ref[...] = out[:HALF]
    send_ref[...] = out[HALF:]
    source, target = iota((FFL, FFL), 0), iota((FFL, FFL), 1)
    y, rest = target // 128, target % 128
    perm = (source == (rest // 16) * 64 + y * 16 + rest % 16).astype(F32).astype(BF16)
    act_y = dot(act, perm).astype(BF16)
    source, target = iota((D, D), 0), iota((D, D), 1)
    y, rest = target // 256, target % 256
    perm = (source == (rest // 32) * 128 + y * 32 + rest % 32).astype(F32).astype(BF16)
    norm_y = dot(tokens(a_ref, b_ref, 0, D), perm).astype(BF16)
    cot = tokens(a_ref, b_ref, PAY, PAY + D)
    gpre = gpre_ref[...]
    for k in range(NY):
        ypay_ref[k, :, :FFL] = gpre
        ypay_ref[k, :, FFL : FFL + 128] = act_y[:, 128 * k : 128 * (k + 1)]
        ypay_ref[k, :, FFL + 128 : 896] = norm_y[:, 256 * k : 256 * (k + 1)]
        ypay_ref[k, :, 896:] = cot


def weight_kernel(in_ref, out_ref):
    rows = NY * TOK
    gpre = in_ref[:, :, :FFL].reshape(rows, FFL)
    act = in_ref[:, :, FFL : FFL + 128].reshape(rows, 128)
    normed = in_ref[:, :, FFL + 128 : 896].reshape(rows, 256)
    cot = in_ref[:, :, 896:].reshape(rows, D)
    up = dot_tn(normed, gpre).astype(BF16)
    down = dot_tn(act, cot).astype(BF16)
    for k in range(FFL // 128):
        cols, more = slice(128 * k, 128 * (k + 1)), slice(FFL + 128 * k, FFL + 128 * (k + 1))
        out_ref[:, 64 * k : 64 * k + 32, :] = up[:, cols].reshape(NZ, 32, 128)
        out_ref[:, 64 * k + 32 : 64 * k + 48, :] = down[:, cols].reshape(NZ, 16, 128)
        out_ref[:, 64 * k + 48 : 64 * k + 64, :] = down[:, more].reshape(NZ, 16, 128)


def add_kernel(a_ref, b_ref, out_ref):
    out_ref[...] = (a_ref[...].astype(F32) + b_ref[...].astype(F32)).astype(BF16)


def mix_grad_kernel(g0_ref, g1_ref, g2_ref, g3_ref, mix_ref, agg_ref, n_ref, ow_ref, gain_ref, _, pay_ref):
    gn = sum(r[...].astype(F32) for r in (g0_ref, g1_ref, g2_ref, g3_ref))
    mix = mix_ref[...]
    scale = lax.rsqrt(jnp.mean(mix * mix, axis=1, keepdims=True) + EPSILON)
    g = gn * gain_ref[...]
    pull = g * scale - mix * (scale * scale * scale * jnp.mean(mix * g, axis=1, keepdims=True))
    half = (n_ref[:, PAY:].astype(F32) + pull).astype(BF16)
    ga = dot_nt(half, ow_ref[...]).astype(BF16)
    hi, mid, low = split3(ga.astype(F32) * agg_ref[...].astype(F32))
    spread = head_spread()
    dots = dot_nt(hi, spread) + dot_nt(mid, spread) + dot_nt(low, spread)
    pay_ref[:, :D] = ga
    pay_ref[:, D:] = pack_parts(dots)


def backward_kernel(
    x_hbm, w_ref, st_ref, eh_ref, score_ref, na_ref, nb_ref, ga_ref, gb_ref, keep_ref, send_ref, chan_ref,
    x_ref, left_ref, right_ref, back_ref, be_ref, z_ref, sg_ref, sems,
):
    chunk = chunks(x_hbm, x_ref, sems, 0)
    for k in range(TOK // 8):
        chunk(k).start()
    st = st_ref[...]
    block = GROUP * CH
    z_ref[...] = jnp.zeros_like(z_ref)
    sg_ref[...] = jnp.zeros_like(sg_ref)
    core = lax.axis_index("core")
    first = core == 0

    @pl.loop(0, TOK // 16)
    def _(it):
        at = pl.ds(pl.multiple_of(it * 8, 8), 8)
        mine, other = ga_ref[at, :D].astype(F32), gb_ref[at, :D].astype(F32)
        ga = jnp.concatenate([jnp.where(first, mine, other), jnp.where(first, other, mine)], axis=0)
        gx = jnp.where(head_select(16), jnp.broadcast_to(ga[:, None, :], (16, HEADS, D)), 0.0)
        gx = gx.reshape(16 * HEADS, D).astype(BF16)
        rows = pl.ds(pl.multiple_of(it * 16 * HEADS, 16 * HEADS), 16 * HEADS)
        right_ref[rows, :] = gx
        back_ref[rows, :] = dot_nt(gx, w_ref[...]).astype(BF16)
        be = dot_nt(gx, eh_ref[...])
        be_ref[rows, :] = jnp.concatenate([be] * GROUP, axis=1)

    @pl.loop(0, TOK // 8)
    def _(it):
        chunk(it).wait()
        rows = pl.ds(pl.multiple_of((it // 2) * 8, 8), 8)
        mine = it % 2 == core
        lse = jnp.where(mine, na_ref[rows, D:PAY].astype(F32), nb_ref[rows, D:PAY].astype(F32))
        lse = as_column(unpack_parts(lse), 8)
        dots = jnp.where(mine, ga_ref[rows, D:].astype(F32), gb_ref[rows, D:].astype(F32))
        dots = as_column(unpack_parts(dots), 8)
        for half in range(2):
            at = pl.multiple_of(it * 2 * block + half * block, block)
            part = slice(half * GROUP * HEADS, (half + 1) * GROUP * HEADS)
            base = pl.ds(
                pl.multiple_of(it * 8 * HEADS + half * GROUP * HEADS, GROUP * HEADS), GROUP * HEADS
            )
            xg = x_ref[pl.ds(at, block), :]
            s = score_ref[:, pl.ds(at, block)]
            sx = jnp.where(same_token(), jnp.concatenate([s] * GROUP, axis=0) - lse[part], -jnp.inf)
            p = jnp.exp(sx)
            head_dots = dot_nt(back_ref[base, :], xg) + be_ref[base, :]
            sg = p * (head_dots - dots[part])
            sg = jnp.sum(sg.reshape(GROUP, HEADS, block), axis=0)
            yz = dot(jnp.concatenate([p, sg], axis=0).astype(BF16), xg)
            left_ref[base, :PIX] = yz[: GROUP * HEADS].astype(BF16)
            z_ref[...] += yz[GROUP * HEADS :]
            sg_ref[...] += sg
            pc = fold(p)
            left_ref[base, PIX:] = jnp.concatenate([pc, pc], axis=1).astype(BF16)

    sg = sg_ref[...]
    sgc = fold(sg)
    last = jnp.concatenate([z_ref[...], sgc, sgc], axis=1)
    tail_hi, tail_low = split2(last)
    out = dot_tn(left_ref[...], right_ref[...]) + dot_tn(tail_hi, st) + dot_tn(tail_low, st)
    for k in range(NX):
        even = out[:PIX, 256 * k : 256 * k + 128]
        odd = out[:PIX, 256 * k + 128 : 256 * (k + 1)]
        keep_ref[k] = jnp.where(core == 0, even, odd).astype(BF16)
        send_ref[k] = jnp.where(core == 0, odd, even).astype(BF16)
    for k in range(NCHAN):
        piece = out[PIX : PIX + CH, 128 * k : 128 * (k + 1)]
        chan_ref[:, 2 * k : 2 * k + 2, :] = piece.reshape(NSPACE, 2, 128).astype(BF16)


def patch_pair_kernel(keep_ref, got_ref, okeep_ref, ogot_ref, *out_refs):
    x = lax.axis_index("x")
    for o, out_ref in enumerate(out_refs):
        to = lax.rem(x + o, NX)
        out_ref[:PIX, :] = (keep_ref[to].astype(F32) + got_ref[to].astype(F32)).astype(BF16)
        rows = pl.ds(pl.multiple_of(to * 8, 8), 8)
        both = okeep_ref[rows, :].astype(F32) + ogot_ref[rows, :].astype(F32)
        for k in range(8):
            out_ref[PIX + 8 * k : PIX + 8 * (k + 1), :] = both[:, 128 * k : 128 * (k + 1)].astype(BF16)


def patch_sum_kernel(p0_ref, p1_ref, p2_ref, p3_ref, chan_ref, mix_ref, out_ref, *refs):
    pay_refs, all_ref = refs[:NY], refs[NY]
    total = sum(r[...].astype(F32) for r in (p0_ref, p1_ref, p2_ref, p3_ref))
    all_ref[:, :, :8, :] = total[:PIX].astype(BF16).reshape(NZ, NY, 8, 128)
    all_ref[:, :, 8:, :] = chan_ref[...].reshape(NZ, NY, 16, 128)
    y = lax.axis_index("y")
    for o, pay_ref in enumerate(pay_refs):
        pay_ref[...] = all_ref[:, pl.ds(lax.rem(y + o, NY), 1)].reshape(NZ, 24, 128)
    x = lax.axis_index("x")
    mix = mix_ref[pl.ds(pl.multiple_of(x * 8, 8), 8), :]
    for k in range(8):
        cols = slice(128 * k, 128 * (k + 1))
        out_ref[:, cols] = (mix[:, cols] + total[PIX + 8 * k : PIX + 8 * (k + 1)]).astype(BF16)


def strip_sum_kernel(p0_ref, p1_ref, p2_ref, p3_ref, z_ref, out_ref):
    total = sum(r[...].astype(F32) for r in (p0_ref, p1_ref, p2_ref, p3_ref))
    out_ref[:, :256, :] = z_ref[...]
    out_ref[:, 256:, :] = total.astype(BF16)


def last_kernel(in_ref, patch_ref, chan_ref, up_ref, down_ref):
    total = jnp.sum(in_ref[...].astype(F32), axis=0)
    for k in range(FFL // 128):
        cols, more = slice(128 * k, 128 * (k + 1)), slice(FFL + 128 * k, FFL + 128 * (k + 1))
        up_ref[:, cols] = total[64 * k : 64 * k + 32]
        down_ref[:, cols] = total[64 * k + 32 : 64 * k + 48]
        down_ref[:, more] = total[64 * k + 48 : 64 * k + 64]
    patch_ref[...] = total[256:264]
    for k in range(8):
        chan_ref[:, 128 * k : 128 * (k + 1)] = total[264 + 2 * k : 266 + 2 * k]


def call(kernel, outs, args, scratch=(), flops=0, nbytes=0, limit=16, hbm=()):
    spaces = [pltpu.HBM if k in hbm else pltpu.VMEM for k in range(len(args))]
    return pl.pallas_call(
        kernel,
        out_shape=[jax.ShapeDtypeStruct(s, d) for s, d in outs],
        in_specs=[pl.BlockSpec(memory_space=space) for space in spaces],
        scratch_shapes=list(scratch),
        cost_estimate=pl.CostEstimate(flops=flops, bytes_accessed=nbytes, transcendentals=0),
        compiler_params=pltpu.CompilerParams(vmem_limit_bytes=limit << 20),
    )(*(pltpu.with_memory_space_constraint(a, pltpu.HBM) if k in hbm else a for k, a in enumerate(args)))


def exchange(x, axes):
    return lax.all_to_all(x, axes, 0, 0, tiled=True)


def swap(x):
    return lax.ppermute(x, "core", [(0, 1), (1, 0)])


def shift(x, o, axis="x", size=NX):
    return lax.ppermute(x, axis, [(i, (i + o) % size) for i in range(size)])


def around(x):
    return [x] + [shift(x, o) for o in range(1, NX)]


def on_device(
    patches, patch_weight, channel_embed, score_map, out_weight, norm_gain, up_weight, down_weight, cotangent
):
    gain = norm_gain.reshape(1, D)
    x = patches.reshape(TOK * CH, PIX)
    score, keep, send, w, st, eh = call(
        forward_kernel,
        [
            ((HEADS, TOK * CH), F32), ((HALF, PAY), BF16), ((HALF, PAY), BF16),
            ((PIX, D), BF16), ((HEADS, D), BF16), ((CH, D), BF16),
        ],
        (x, patch_weight, score_map.T, channel_embed),
        [
            pltpu.VMEM((TOK * CH, PIX), BF16),
            pltpu.VMEM((CH, D), F32),
            pltpu.VMEM((TOK * HEADS, PIX), BF16),
            pltpu.VMEM((TOK * HEADS, CH), BF16),
            pltpu.VMEM((TOK, 128), F32),
            pltpu.SemaphoreType.DMA((3 + TOK // 8,)),
        ],
        flops=4 << 30, nbytes=4 << 20, limit=24, hbm=(0, 1, 2, 3),
    )
    (pay,) = call(
        pair_kernel, [((HALF + 8, PAY), BF16)], (keep, swap(send), cotangent[0]),
        flops=1 << 29, nbytes=1 << 18,
    )
    npay, agg, mix = call(
        combine_kernel,
        [((HALF, PAY + D), BF16), ((HALF, D), BF16), ((HALF, D), F32)],
        (*around(pay), out_weight, gain),
        flops=1 << 30, nbytes=3 << 20,
    )
    nother = swap(npay)
    act, gpre, gkeep, gsend = call(
        mlp_kernel,
        [((TOK, FFL), BF16), ((TOK, FFL), BF16), ((HALF, D), BF16), ((HALF, D), BF16)],
        (npay, nother, up_weight, down_weight),
        flops=1 << 30, nbytes=3 << 20,
    )
    (gsum,) = call(
        add_kernel, [((HALF, D), BF16)], (gkeep, swap(gsend)), flops=1 << 20, nbytes=1 << 18
    )
    okeep, osend, ypay = call(
        mlp_out_kernel,
        [((HALF, D), BF16), ((HALF, D), BF16), ((NY, TOK, 896 + D), BF16)],
        (npay, nother, act, gpre, down_weight),
        flops=1 << 30, nbytes=3 << 20,
    )
    ogot = swap(osend)
    yfull = exchange(ypay, ("y",))
    (gpay,) = call(
        mix_grad_kernel, [((HALF, PAY), BF16)],
        (*around(gsum), mix, agg, npay, out_weight, gain, okeep),
        flops=1 << 30, nbytes=3 << 20,
    )
    gother = swap(gpay)
    pkeep, psend, chan = call(
        backward_kernel,
        [((NX, PIX, 128), BF16), ((NX, PIX, 128), BF16), ((NSPACE, 16, 128), BF16)],
        (x, w, st, eh, score, npay, nother, gpay, gother),
        [
            pltpu.VMEM((TOK * CH, PIX), BF16),
            pltpu.VMEM((TOK * HEADS, PIX + 128), BF16),
            pltpu.VMEM((TOK * HEADS, D), BF16),
            pltpu.VMEM((TOK * HEADS, PIX), BF16),
            pltpu.VMEM((TOK * HEADS, PIX), F32),
            pltpu.VMEM((HEADS, PIX), F32),
            pltpu.VMEM((HEADS, GROUP * CH), F32),
            pltpu.SemaphoreType.DMA((TOK // 8,)),
        ],
        flops=4 << 30, nbytes=6 << 20, limit=24, hbm=(0,),
    )
    own, *away = call(
        patch_pair_kernel, [((PIX + 64, 128), BF16)] * NX, (pkeep, swap(psend), okeep, ogot),
        flops=1 << 20, nbytes=1 << 20,
    )
    layer_out, strip, *strips = call(
        patch_sum_kernel,
        [((8, D), BF16)] + [((NZ, 24, 128), BF16)] * NY,
        (own, *[shift(v, o) for o, v in enumerate(away, 1)], chan, mix),
        [pltpu.VMEM((NZ, NY, 24, 128), BF16)],
        flops=1 << 20, nbytes=1 << 20,
    )
    (zpay,) = call(
        weight_kernel, [((NZ, 256, 128), BF16)], (yfull,), flops=1 << 28, nbytes=3 << 20
    )
    (spay,) = call(
        strip_sum_kernel, [((NZ, 280, 128), BF16)],
        (strip, *[shift(v, o, "y", NY) for o, v in enumerate(strips, 1)], zpay),
        flops=1 << 20, nbytes=1 << 20,
    )
    patch_grad, channel_grad, up_grad, down_grad = call(
        last_kernel,
        [((8, 128), F32), ((2, D), F32), ((32, FFL), F32), ((16, D), F32)],
        (exchange(spay, ("z",)),),
        flops=1 << 20, nbytes=1 << 20,
    )
    return layer_out[None], up_grad, down_grad, patch_grad, channel_grad


def solution(mesh):
    fine = Mesh(np.asarray(mesh.devices).reshape(4, 2, NZ, NY), ("x", "core", "z", "y"))
    return jax.shard_map(
        on_device,
        mesh=fine,
        in_specs=(
            P(SPACE, None, CHAN, None),
            P(),
            P(CHAN, None),
            P(),
            P(),
            P(),
            P(None, CHAN),
            P(CHAN, None),
            P(SPACE, CHAN, None),
        ),
        out_specs=(
            P(SPACE, CHAN, None),
            P(SPACE, CHAN),
            P((*CHAN, *SPACE), None),
            P(SPACE, CHAN),
            P((*CHAN, *SPACE), None),
        ),
        check_vma=False,
    )
```

```python
import functools

import jax
import jax.numpy as jnp
import numpy as np
from jax import lax
from jax.experimental import pallas as pl
from jax.experimental.pallas import tpu as pltpu
from jax.sharding import Mesh
from jax.sharding import PartitionSpec as P

EPSILON = 1e-06
F32, BF16 = jnp.float32, jnp.bfloat16
TOK, CH, PIX, D, HEADS, HS = 64, 64, 256, 1024, 16, 64
FFL = 512
PAY = D + 128
GROUP = 4
CHAN, SPACE = ("x", "core"), ("z", "y")
NCHAN, NSPACE, NX, NY, NZ = 8, 32, 4, 4, 8
HALF = TOK // 2


def dot(a, b):
    return lax.dot_general(a, b, (((1,), (0,)), ((), ())), preferred_element_type=F32)


def dot_nt(a, b):
    return lax.dot_general(a, b, (((1,), (1,)), ((), ())), preferred_element_type=F32)


def dot_tn(a, b):
    return lax.dot_general(a, b, (((0,), (0,)), ((), ())), preferred_element_type=F32)


def iota(shape, dim):
    return lax.broadcasted_iota(jnp.int32, shape, dim)


def split2(x):
    hi = x.astype(BF16)
    return hi, (x - hi.astype(F32)).astype(BF16)


def split3(x):
    hi = x.astype(BF16)
    rest = x - hi.astype(F32)
    mid = rest.astype(BF16)
    low = (rest - mid.astype(F32)).astype(BF16)
    return hi, mid, low


def head_select(rows):
    shape = (rows, HEADS, D)
    return iota(shape, 2) >> 6 == iota(shape, 1)


def head_spread():
    shape = (128, D)
    return (iota(shape, 1) >> 6 == iota(shape, 0)).astype(F32).astype(BF16)


def pack_parts(x):
    lane = iota(x.shape, 1)
    x = jnp.where(lane < HEADS, x, 0.0)
    hi, mid, low = (v.astype(F32) for v in split3(x))
    return (hi + pltpu.roll(mid, HEADS, 1) + pltpu.roll(low, 2 * HEADS, 1)).astype(BF16)


def unpack_parts(x):
    x = x.astype(F32)
    whole = x + pltpu.roll(x, 128 - HEADS, 1) + pltpu.roll(x, 128 - 2 * HEADS, 1)
    return jnp.where(iota(x.shape, 1) < HEADS, whole, 0.0)


def as_column(x, rows):
    shape = (rows, HEADS, 128)
    mask = iota(shape, 2) == iota(shape, 1)
    picked = jnp.where(mask, jnp.broadcast_to(x[:, None, :], shape), 0.0)
    return jnp.sum(picked, axis=2, keepdims=True).reshape(rows * HEADS, 1)


def as_lanes(col, rows):
    shape = (rows, HEADS, 128)
    mask = iota(shape, 2) == iota(shape, 1)
    full = jnp.broadcast_to(col, (rows * HEADS, 128)).reshape(shape)
    return jnp.sum(jnp.where(mask, full, 0.0), axis=1)


def fold(x):
    return x[:, :CH] + x[:, CH : 2 * CH] + x[:, 2 * CH : 3 * CH] + x[:, 3 * CH :]


def same_token():
    shape = (GROUP * HEADS, GROUP * CH)
    return iota(shape, 0) >> 4 == iota(shape, 1) >> 6


def chunks(src, dst, sems, first):
    size = 8 * CH

    def chunk(k):
        rows = pl.ds(pl.multiple_of(k * size, size), size)
        return pltpu.make_async_copy(src.at[rows, :], dst.at[rows, :], sems.at[first + k])

    return chunk


def forward_kernel(
    x_hbm, w_hbm, st_hbm, e_hbm, score_ref, keep_ref, send_ref, w_ref, st_ref, eh_ref,
    x_ref, e_ref, y_ref, p_ref, lane_ref, sems,
):
    loads = [
        pltpu.make_async_copy(src, dst, sems.at[k])
        for k, (src, dst) in enumerate(((st_hbm, st_ref), (w_hbm, w_ref), (e_hbm, e_ref)))
    ]
    for copy in loads:
        copy.start()
    block = GROUP * CH
    octet = 2 * block
    chunk = chunks(x_hbm, x_ref, sems, 3)
    for k in range(TOK // 8):
        chunk(k).start()
    for copy in loads:
        copy.wait()
    st = st_ref[...]
    w2 = jnp.concatenate(split2(dot_nt(st, w_ref[...])), axis=0)
    e_hi, e_low = split2(e_ref[...])
    eh_ref[...] = e_hi
    es = dot_nt(st, e_hi) + dot_nt(st, e_low)
    es4 = jnp.concatenate([es] * GROUP, axis=1)
    core = lax.axis_index("core")

    wide = 4

    @pl.loop(0, TOK // 8 // wide)
    def _(it):
        for k in range(wide):
            chunk(it * wide + k).wait()
        spots = [pl.multiple_of((it * wide * 2 + k) * block, block) for k in range(2 * wide)]
        xs = [x_ref[pl.ds(at, block), :] for at in spots]
        twos = [dot_nt(w2, xg) for xg in xs]
        ss = [s2[:HEADS] + s2[HEADS:] + es4 for s2 in twos]
        for at, s in zip(spots, ss):
            score_ref[:, pl.ds(at, block)] = s
        mask = same_token()
        sx = [jnp.where(mask, jnp.concatenate([s] * GROUP, axis=0), -jnp.inf) for s in ss]
        tops = [jnp.max(s, axis=1, keepdims=True) for s in sx]
        ws = [jnp.exp(s - m) for s, m in zip(sx, tops)]
        totals = [jnp.sum(w, axis=1, keepdims=True) for w in ws]
        ws = [w * (1.0 / total) for w, total in zip(ws, totals)]
        ys = [dot(w.astype(BF16), xg) for w, xg in zip(ws, xs)]
        cols = [m + jnp.log(total) for m, total in zip(tops, totals)]
        for k, (y, w) in enumerate(zip(ys, ws)):
            rows = GROUP * HEADS
            rows = pl.ds(pl.multiple_of((it * wide * 2 + k) * rows, rows), rows)
            y_ref[rows, :] = y.astype(BF16)
            p_ref[rows, :] = fold(w).astype(BF16)
        size = 8 * wide
        lane_ref[pl.ds(pl.multiple_of(it * size, size), size), :] = as_lanes(
            jnp.concatenate(cols, axis=0), size
        )

    @pl.loop(0, TOK // 16, unroll=2)
    def _(it):
        rows = pl.ds(pl.multiple_of(it * 16 * HEADS, 16 * HEADS), 16 * HEADS)
        out = dot(y_ref[rows, :], w_ref[...]) + dot(p_ref[rows, :], eh_ref[...])
        out = jnp.where(head_select(16), out.reshape(16, HEADS, D), 0.0)
        out = jnp.sum(out, axis=1)
        parts = lane_ref[pl.ds(pl.multiple_of(it * 16, 16), 16), :]
        first = core == 0
        to = pl.ds(pl.multiple_of(it * 8, 8), 8)
        keep_ref[to, :D] = jnp.where(first, out[:8], out[8:]).astype(BF16)
        send_ref[to, :D] = jnp.where(first, out[8:], out[:8]).astype(BF16)
        keep_ref[to, D:] = pack_parts(jnp.where(first, parts[:8], parts[8:]))
        send_ref[to, D:] = pack_parts(jnp.where(first, parts[8:], parts[:8]))


def merge(outs, parts):
    rows = outs[0].shape[0]
    lses = [unpack_parts(p) for p in parts]
    top = functools.reduce(jnp.maximum, lses)
    es = [jnp.exp(v - top) for v in lses]
    total = sum(es)
    weight = jnp.concatenate([e / total for e in es], axis=0)
    hi, low = split2(weight)
    spread = head_spread()
    wide = dot(hi, spread) + dot(low, spread)
    out = sum(o.astype(F32) * wide[k * rows : (k + 1) * rows] for k, o in enumerate(outs))
    return out, top + jnp.log(total)


def pair_kernel(keep_ref, got_ref, cot_ref, pay_ref):
    out, lse = merge([keep_ref[:, :D], got_ref[:, :D]], [keep_ref[:, D:], got_ref[:, D:]])
    pay_ref[:HALF, :D] = out.astype(BF16)
    pay_ref[:HALF, D:] = pack_parts(lse)
    pay_ref[HALF:, :D] = cot_ref[...]
    pay_ref[HALF:, D:] = jnp.zeros((8, 128), BF16)


def combine_kernel(p0_ref, p1_ref, p2_ref, p3_ref, ow_ref, gain_ref, pay_ref, agg_ref, mix_ref):
    refs = (p0_ref, p1_ref, p2_ref, p3_ref)
    out, lse = merge([r[:HALF, :D] for r in refs], [r[:HALF, D:] for r in refs])
    agg = out.astype(BF16)
    mix = dot(agg, ow_ref[...])
    scale = lax.rsqrt(jnp.mean(mix * mix, axis=1, keepdims=True) + EPSILON)
    pay_ref[:, :D] = (mix * scale * gain_ref[...]).astype(BF16)
    pay_ref[:, D:PAY] = pack_parts(lse)
    x = lax.axis_index("x")
    for k in range(NX):
        rows = pl.ds(pl.multiple_of(lax.rem(x + (NX - k), NX) * 8, 8), 8)
        pay_ref[rows, PAY:] = refs[k][HALF:, :D]
    agg_ref[...] = agg
    mix_ref[...] = mix


def tokens(a_ref, b_ref, start, stop):
    return jnp.concatenate([a_ref[:, start:stop], b_ref[:, start:stop]], axis=0)


def mlp_kernel(a_ref, b_ref, up_ref, down_ref, act_ref, gpre_ref, keep_ref, send_ref):
    normed = tokens(a_ref, b_ref, 0, D)
    cot = tokens(a_ref, b_ref, PAY, PAY + D)
    x = dot(normed, up_ref[...])
    c = np.float32(np.sqrt(2 / np.pi))
    t = jnp.tanh(c * (x + 0.044715 * (x * x * x)))
    act_ref[...] = (0.5 * x * (1.0 + t)).astype(BF16)
    slope = 0.5 * (1.0 + t) + 0.5 * x * (1.0 - t * t) * (c * (1.0 + (3 * 0.044715) * (x * x)))
    gpre = (dot_nt(cot, down_ref[...]) * slope).astype(BF16)
    gpre_ref[...] = gpre
    gn = dot_nt(gpre, up_ref[...]).astype(BF16)
    keep_ref[...] = gn[:HALF]
    send_ref[...] = gn[HALF:]


def mlp_out_kernel(a_ref, b_ref, act_ref, gpre_ref, down_ref, _, keep_ref, send_ref, ypay_ref):
    act = act_ref[...]
    out = dot(act, down_ref[...]).astype(BF16)
    keep_ref[...] = out[:HALF]
    send_ref[...] = out[HALF:]
    source, target = iota((FFL, FFL), 0), iota((FFL, FFL), 1)
    y, rest = target >> 7, target & 127
    perm = (source == ((rest >> 4) << 6) + (y << 4) + (rest & 15)).astype(F32).astype(BF16)
    act_y = dot(act, perm).astype(BF16)
    source, target = iota((D, D), 0), iota((D, D), 1)
    y, rest = target >> 8, target & 255
    perm = (source == ((rest >> 5) << 7) + (y << 5) + (rest & 31)).astype(F32).astype(BF16)
    norm_y = dot(tokens(a_ref, b_ref, 0, D), perm).astype(BF16)
    cot = tokens(a_ref, b_ref, PAY, PAY + D)
    gpre = gpre_ref[...]
    for k in range(NY):
        ypay_ref[k, :, :FFL] = gpre
        ypay_ref[k, :, FFL : FFL + 128] = act_y[:, 128 * k : 128 * (k + 1)]
        ypay_ref[k, :, FFL + 128 : 896] = norm_y[:, 256 * k : 256 * (k + 1)]
        ypay_ref[k, :, 896:] = cot


def weight_kernel(in_ref, out_ref):
    rows = NY * TOK
    gpre = in_ref[:, :, :FFL].reshape(rows, FFL)
    act = in_ref[:, :, FFL : FFL + 128].reshape(rows, 128)
    normed = in_ref[:, :, FFL + 128 : 896].reshape(rows, 256)
    cot = in_ref[:, :, 896:].reshape(rows, D)
    up = dot_tn(normed, gpre).astype(BF16)
    down = dot_tn(act, cot).astype(BF16)
    for k in range(FFL // 128):
        cols, more = slice(128 * k, 128 * (k + 1)), slice(FFL + 128 * k, FFL + 128 * (k + 1))
        out_ref[:, 64 * k : 64 * k + 32, :] = up[:, cols].reshape(NZ, 32, 128)
        out_ref[:, 64 * k + 32 : 64 * k + 48, :] = down[:, cols].reshape(NZ, 16, 128)
        out_ref[:, 64 * k + 48 : 64 * k + 64, :] = down[:, more].reshape(NZ, 16, 128)


def add_kernel(a_ref, b_ref, out_ref):
    out_ref[...] = (a_ref[...].astype(F32) + b_ref[...].astype(F32)).astype(BF16)


def mix_grad_kernel(g0_ref, g1_ref, g2_ref, g3_ref, mix_ref, agg_ref, n_ref, ow_ref, gain_ref, pay_ref):
    gn = sum(r[...].astype(F32) for r in (g0_ref, g1_ref, g2_ref, g3_ref))
    mix = mix_ref[...]
    scale = lax.rsqrt(jnp.mean(mix * mix, axis=1, keepdims=True) + EPSILON)
    g = gn * gain_ref[...]
    pull = g * scale - mix * (scale * scale * scale * jnp.mean(mix * g, axis=1, keepdims=True))
    half = (n_ref[:, PAY:].astype(F32) + pull).astype(BF16)
    ga = dot_nt(half, ow_ref[...]).astype(BF16)
    hi, mid, low = split3(ga.astype(F32) * agg_ref[...].astype(F32))
    spread = head_spread()
    dots = dot_nt(hi, spread) + dot_nt(mid, spread) + dot_nt(low, spread)
    pay_ref[:, :D] = ga
    pay_ref[:, D:] = pack_parts(dots)


def backward_kernel(
    x_ref, w_ref, st_ref, eh_ref, score_ref, na_ref, nb_ref, ga_ref, gb_ref, keep_ref, send_ref, chan_ref,
    left_ref, right_ref, back_ref, be_ref, z_ref, sg_ref,
):
    st = st_ref[...]
    block = GROUP * CH
    z_ref[...] = jnp.zeros_like(z_ref)
    sg_ref[...] = jnp.zeros_like(sg_ref)
    core = lax.axis_index("core")
    first = core == 0

    @pl.loop(0, TOK // 16)
    def _(it):
        at = pl.ds(pl.multiple_of(it * 8, 8), 8)
        mine, other = ga_ref[at, :D].astype(F32), gb_ref[at, :D].astype(F32)
        ga = jnp.concatenate([jnp.where(first, mine, other), jnp.where(first, other, mine)], axis=0)
        gx = jnp.where(head_select(16), jnp.broadcast_to(ga[:, None, :], (16, HEADS, D)), 0.0)
        gx = gx.reshape(16 * HEADS, D).astype(BF16)
        rows = pl.ds(pl.multiple_of(it * 16 * HEADS, 16 * HEADS), 16 * HEADS)
        right_ref[rows, :] = gx
        back_ref[rows, :] = dot_nt(gx, w_ref[...]).astype(BF16)
        be = dot_nt(gx, eh_ref[...])
        be_ref[rows, :] = jnp.concatenate([be] * GROUP, axis=1)

    wide = 2

    @pl.loop(0, TOK // 8 // wide)
    def _(it):
        size = GROUP * HEADS
        lses, dots = [], []
        for k in range(wide):
            octet = it * wide + k
            rows = pl.ds(pl.multiple_of((octet // 2) * 8, 8), 8)
            mine = octet % 2 == core
            lse = jnp.where(mine, na_ref[rows, D:PAY].astype(F32), nb_ref[rows, D:PAY].astype(F32))
            lse = as_column(unpack_parts(lse), 8)
            dot_ = jnp.where(mine, ga_ref[rows, D:].astype(F32), gb_ref[rows, D:].astype(F32))
            dot_ = as_column(unpack_parts(dot_), 8)
            lses += [lse[:size], lse[size:]]
            dots += [dot_[:size], dot_[size:]]
        spots = [pl.multiple_of((it * wide * 2 + k) * block, block) for k in range(2 * wide)]
        bases = [pl.ds(pl.multiple_of((it * wide * 2 + k) * size, size), size) for k in range(2 * wide)]
        xs = [x_ref[pl.ds(at, block), :] for at in spots]
        heads = [dot_nt(back_ref[base, :], xg) + be_ref[base, :] for base, xg in zip(bases, xs)]
        ss = [score_ref[:, pl.ds(at, block)] for at in spots]
        mask = same_token()
        sx = [
            jnp.where(mask, jnp.concatenate([s] * GROUP, axis=0) - lse, -jnp.inf)
            for s, lse in zip(ss, lses)
        ]
        ps = [jnp.exp(s) for s in sx]
        sgs = [p * (head - d) for p, head, d in zip(ps, heads, dots)]
        sgs = [jnp.sum(sg.reshape(GROUP, HEADS, block), axis=0) for sg in sgs]
        yzs = [
            dot(jnp.concatenate([p, sg], axis=0).astype(BF16), xg) for p, sg, xg in zip(ps, sgs, xs)
        ]
        for base, yz, p in zip(bases, yzs, ps):
            left_ref[base, :PIX] = yz[:size].astype(BF16)
            pc = fold(p)
            left_ref[base, PIX:] = jnp.concatenate([pc, pc], axis=1).astype(BF16)
        z_ref[...] += sum(yz[size:] for yz in yzs)
        sg_ref[...] += sum(sgs)

    sg = sg_ref[...]
    sgc = fold(sg)
    last = jnp.concatenate([z_ref[...], sgc, sgc], axis=1)
    tail_hi, tail_low = split2(last)
    out = dot_tn(left_ref[...], right_ref[...]) + dot_tn(tail_hi, st) + dot_tn(tail_low, st)
    for k in range(NX):
        even = out[:PIX, 256 * k : 256 * k + 128]
        odd = out[:PIX, 256 * k + 128 : 256 * (k + 1)]
        keep_ref[k] = jnp.where(core == 0, even, odd).astype(BF16)
        send_ref[k] = jnp.where(core == 0, odd, even).astype(BF16)
    for k in range(NCHAN):
        piece = out[PIX : PIX + CH, 128 * k : 128 * (k + 1)]
        chan_ref[:, 2 * k : 2 * k + 2, :] = piece.reshape(NSPACE, 2, 128).astype(BF16)


def patch_pair_kernel(keep_ref, got_ref, okeep_ref, ogot_ref, *out_refs):
    x = lax.axis_index("x")
    for o, out_ref in enumerate(out_refs):
        to = lax.rem(x + o, NX)
        out_ref[:PIX, :] = (keep_ref[to].astype(F32) + got_ref[to].astype(F32)).astype(BF16)
        rows = pl.ds(pl.multiple_of(to * 8, 8), 8)
        both = okeep_ref[rows, :].astype(F32) + ogot_ref[rows, :].astype(F32)
        for k in range(8):
            out_ref[PIX + 8 * k : PIX + 8 * (k + 1), :] = both[:, 128 * k : 128 * (k + 1)].astype(BF16)


def patch_sum_kernel(p0_ref, p1_ref, p2_ref, p3_ref, chan_ref, mix_ref, out_ref, *refs):
    pay_refs, all_ref = refs[:NY], refs[NY]
    total = sum(r[...].astype(F32) for r in (p0_ref, p1_ref, p2_ref, p3_ref))
    all_ref[:, :, :8, :] = total[:PIX].astype(BF16).reshape(NZ, NY, 8, 128)
    all_ref[:, :, 8:, :] = chan_ref[...].reshape(NZ, NY, 16, 128)
    y = lax.axis_index("y")
    for o, pay_ref in enumerate(pay_refs):
        pay_ref[...] = all_ref[:, pl.ds(lax.rem(y + o, NY), 1)].reshape(NZ, 24, 128)
    x = lax.axis_index("x")
    mix = mix_ref[pl.ds(pl.multiple_of(x * 8, 8), 8), :]
    for k in range(8):
        cols = slice(128 * k, 128 * (k + 1))
        out_ref[:, cols] = (mix[:, cols] + total[PIX + 8 * k : PIX + 8 * (k + 1)]).astype(BF16)


def strip_sum_kernel(p0_ref, p1_ref, p2_ref, p3_ref, z_ref, out_ref):
    total = sum(r[...].astype(F32) for r in (p0_ref, p1_ref, p2_ref, p3_ref))
    out_ref[:, :256, :] = z_ref[...]
    out_ref[:, 256:, :] = total.astype(BF16)


def last_kernel(in_ref, patch_ref, chan_ref, up_ref, down_ref):
    total = jnp.sum(in_ref[...].astype(F32), axis=0)
    for k in range(FFL // 128):
        cols, more = slice(128 * k, 128 * (k + 1)), slice(FFL + 128 * k, FFL + 128 * (k + 1))
        up_ref[:, cols] = total[64 * k : 64 * k + 32]
        down_ref[:, cols] = total[64 * k + 32 : 64 * k + 48]
        down_ref[:, more] = total[64 * k + 48 : 64 * k + 64]
    patch_ref[...] = total[256:264]
    for k in range(8):
        chan_ref[:, 128 * k : 128 * (k + 1)] = total[264 + 2 * k : 266 + 2 * k]


def call(kernel, outs, args, scratch=(), flops=0, nbytes=0, limit=16, hbm=()):
    spaces = [pltpu.HBM if k in hbm else pltpu.VMEM for k in range(len(args))]
    return pl.pallas_call(
        kernel,
        out_shape=[jax.ShapeDtypeStruct(s, d) for s, d in outs],
        in_specs=[pl.BlockSpec(memory_space=space) for space in spaces],
        scratch_shapes=list(scratch),
        cost_estimate=pl.CostEstimate(flops=flops, bytes_accessed=nbytes, transcendentals=0),
        compiler_params=pltpu.CompilerParams(vmem_limit_bytes=limit << 20),
    )(*(pltpu.with_memory_space_constraint(a, pltpu.HBM) if k in hbm else a for k, a in enumerate(args)))


def exchange(x, axes):
    return lax.all_to_all(x, axes, 0, 0, tiled=True)


def swap(x):
    return lax.ppermute(x, "core", [(0, 1), (1, 0)])


def shift(x, o, axis="x", size=NX):
    return lax.ppermute(x, axis, [(i, (i + o) % size) for i in range(size)])


def around(x):
    return [x] + [shift(x, o) for o in range(1, NX)]


def forward(x, patch_weight, st, channel_embed):
    return call(
        forward_kernel,
        [
            ((HEADS, TOK * CH), F32), ((HALF, PAY), BF16), ((HALF, PAY), BF16),
            ((PIX, D), BF16), ((HEADS, D), BF16), ((CH, D), BF16),
        ],
        (x, patch_weight, st, channel_embed),
        [
            pltpu.VMEM((TOK * CH, PIX), BF16),
            pltpu.VMEM((CH, D), F32),
            pltpu.VMEM((TOK * HEADS, PIX), BF16),
            pltpu.VMEM((TOK * HEADS, CH), BF16),
            pltpu.VMEM((TOK, 128), F32),
            pltpu.SemaphoreType.DMA((3 + TOK // 8,)),
        ],
        flops=4 << 30, nbytes=4 << 20, limit=24, hbm=(0, 1, 2, 3),
    )


def backward(x, w, st, eh, score, npay, nother, gpay, gother):
    return call(
        backward_kernel,
        [((NX, PIX, 128), BF16), ((NX, PIX, 128), BF16), ((NSPACE, 16, 128), BF16)],
        (x, w, st, eh, score, npay, nother, gpay, gother),
        [
            pltpu.VMEM((TOK * HEADS, PIX + 128), BF16),
            pltpu.VMEM((TOK * HEADS, D), BF16),
            pltpu.VMEM((TOK * HEADS, PIX), BF16),
            pltpu.VMEM((TOK * HEADS, PIX), F32),
            pltpu.VMEM((HEADS, PIX), F32),
            pltpu.VMEM((HEADS, GROUP * CH), F32),
        ],
        flops=2 << 30, nbytes=1 << 20, limit=24,
    )


def on_device(
    patches, patch_weight, channel_embed, score_map, out_weight, norm_gain, up_weight, down_weight, cotangent
):
    gain = norm_gain.reshape(1, D)
    x = patches.reshape(TOK * CH, PIX)
    score, keep, send, w, st, eh = forward(x, patch_weight, score_map.T, channel_embed)
    (pay,) = call(
        pair_kernel, [((HALF + 8, PAY), BF16)], (keep, swap(send), cotangent[0]),
        flops=1 << 29, nbytes=1 << 18,
    )
    npay, agg, mix = call(
        combine_kernel,
        [((HALF, PAY + D), BF16), ((HALF, D), BF16), ((HALF, D), F32)],
        (*around(pay), out_weight, gain),
        flops=1 << 30, nbytes=3 << 20,
    )
    nother = swap(npay)
    act, gpre, gkeep, gsend = call(
        mlp_kernel,
        [((TOK, FFL), BF16), ((TOK, FFL), BF16), ((HALF, D), BF16), ((HALF, D), BF16)],
        (npay, nother, up_weight, down_weight),
        flops=1 << 30, nbytes=3 << 20,
    )
    (gsum,) = call(
        add_kernel, [((HALF, D), BF16)], (gkeep, swap(gsend)), flops=1 << 20, nbytes=1 << 18
    )
    okeep, osend, ypay = call(
        mlp_out_kernel,
        [((HALF, D), BF16), ((HALF, D), BF16), ((NY, TOK, 896 + D), BF16)],
        (npay, nother, act, gpre, down_weight, gsum),
        flops=1 << 30, nbytes=3 << 20,
    )
    ogot = swap(osend)
    yfull = exchange(ypay, ("y",))
    (gpay,) = call(
        mix_grad_kernel, [((HALF, PAY), BF16)],
        (*around(gsum), mix, agg, npay, out_weight, gain),
        flops=1 << 30, nbytes=3 << 20,
    )
    gother = swap(gpay)
    pkeep, psend, chan = backward(x, w, st, eh, score, npay, nother, gpay, gother)
    own, *away = call(
        patch_pair_kernel, [((PIX + 64, 128), BF16)] * NX, (pkeep, swap(psend), okeep, ogot),
        flops=1 << 20, nbytes=1 << 20,
    )
    layer_out, strip, *strips = call(
        patch_sum_kernel,
        [((8, D), BF16)] + [((NZ, 24, 128), BF16)] * NY,
        (own, *[shift(v, o) for o, v in enumerate(away, 1)], chan, mix),
        [pltpu.VMEM((NZ, NY, 24, 128), BF16)],
        flops=1 << 20, nbytes=1 << 20,
    )
    (zpay,) = call(
        weight_kernel, [((NZ, 256, 128), BF16)], (yfull,), flops=1 << 28, nbytes=3 << 20
    )
    (spay,) = call(
        strip_sum_kernel, [((NZ, 280, 128), BF16)],
        (strip, *[shift(v, o, "y", NY) for o, v in enumerate(strips, 1)], zpay),
        flops=1 << 20, nbytes=1 << 20,
    )
    patch_grad, channel_grad, up_grad, down_grad = call(
        last_kernel,
        [((8, 128), F32), ((2, D), F32), ((32, FFL), F32), ((16, D), F32)],
        (exchange(spay, ("z",)),),
        flops=1 << 20, nbytes=1 << 20,
    )
    return layer_out[None], up_grad, down_grad, patch_grad, channel_grad


def solution(mesh):
    fine = Mesh(np.asarray(mesh.devices).reshape(4, 2, NZ, NY), ("x", "core", "z", "y"))
    return jax.shard_map(
        on_device,
        mesh=fine,
        in_specs=(
            P(SPACE, None, CHAN, None),
            P(),
            P(CHAN, None),
            P(),
            P(),
            P(),
            P(None, CHAN),
            P(CHAN, None),
            P(SPACE, CHAN, None),
        ),
        out_specs=(
            P(SPACE, CHAN, None),
            P(SPACE, CHAN),
            P((*CHAN, *SPACE), None),
            P(SPACE, CHAN),
            P((*CHAN, *SPACE), None),
        ),
        check_vma=False,
    )
```

```python
import functools

import jax
import jax.numpy as jnp
import numpy as np
from jax import lax
from jax.experimental import pallas as pl
from jax.experimental.pallas import tpu as pltpu
from jax.sharding import Mesh
from jax.sharding import PartitionSpec as P

EPSILON = 1e-06
F32, BF16 = jnp.float32, jnp.bfloat16
TOK, CH, PIX, D, HEADS, HS = 64, 64, 256, 1024, 16, 64
FFL = 512
PAY = D + 128
GROUP = 4
CHAN, SPACE, NEAR = ("x", "core"), ("far", "low", "y"), ("low", "y")
NCHAN, NSPACE, NX, NNEAR, NFAR = 8, 32, 4, 8, 4
YPAY = 1792
HALF = TOK // 2


def dot(a, b):
    return lax.dot_general(a, b, (((1,), (0,)), ((), ())), preferred_element_type=F32)


def dot_nt(a, b):
    return lax.dot_general(a, b, (((1,), (1,)), ((), ())), preferred_element_type=F32)


def dot_tn(a, b):
    return lax.dot_general(a, b, (((0,), (0,)), ((), ())), preferred_element_type=F32)


def iota(shape, dim):
    return lax.broadcasted_iota(jnp.int32, shape, dim)


def split2(x):
    hi = x.astype(BF16)
    return hi, (x - hi.astype(F32)).astype(BF16)


def split3(x):
    hi = x.astype(BF16)
    rest = x - hi.astype(F32)
    mid = rest.astype(BF16)
    low = (rest - mid.astype(F32)).astype(BF16)
    return hi, mid, low


def head_select(rows):
    shape = (rows, HEADS, D)
    return iota(shape, 2) >> 6 == iota(shape, 1)


def head_spread():
    shape = (128, D)
    return (iota(shape, 1) >> 6 == iota(shape, 0)).astype(F32).astype(BF16)


def pack_parts(x):
    lane = iota(x.shape, 1)
    x = jnp.where(lane < HEADS, x, 0.0)
    hi, mid, low = (v.astype(F32) for v in split3(x))
    return (hi + pltpu.roll(mid, HEADS, 1) + pltpu.roll(low, 2 * HEADS, 1)).astype(BF16)


def unpack_parts(x):
    x = x.astype(F32)
    whole = x + pltpu.roll(x, 128 - HEADS, 1) + pltpu.roll(x, 128 - 2 * HEADS, 1)
    return jnp.where(iota(x.shape, 1) < HEADS, whole, 0.0)


def as_column(x, rows):
    shape = (rows, HEADS, 128)
    mask = iota(shape, 2) == iota(shape, 1)
    picked = jnp.where(mask, jnp.broadcast_to(x[:, None, :], shape), 0.0)
    return jnp.sum(picked, axis=2, keepdims=True).reshape(rows * HEADS, 1)


def as_lanes(col, rows):
    shape = (rows, HEADS, 128)
    mask = iota(shape, 2) == iota(shape, 1)
    full = jnp.broadcast_to(col, (rows * HEADS, 128)).reshape(shape)
    return jnp.sum(jnp.where(mask, full, 0.0), axis=1)


def fold(x):
    return x[:, :CH] + x[:, CH : 2 * CH] + x[:, 2 * CH : 3 * CH] + x[:, 3 * CH :]


def same_token():
    shape = (GROUP * HEADS, GROUP * CH)
    return iota(shape, 0) >> 4 == iota(shape, 1) >> 6


def chunks(src, dst, sems, first):
    size = 8 * CH

    def chunk(k):
        rows = pl.ds(pl.multiple_of(k * size, size), size)
        return pltpu.make_async_copy(src.at[rows, :], dst.at[rows, :], sems.at[first + k])

    return chunk


def forward_kernel(
    x_hbm, w_hbm, st_hbm, e_hbm, score_ref, keep_ref, send_ref, w_ref, st_ref, eh_ref,
    x_ref, e_ref, y_ref, p_ref, lane_ref, sems,
):
    loads = [
        pltpu.make_async_copy(src, dst, sems.at[k])
        for k, (src, dst) in enumerate(((st_hbm, st_ref), (w_hbm, w_ref), (e_hbm, e_ref)))
    ]
    for copy in loads:
        copy.start()
    block = GROUP * CH
    octet = 2 * block
    chunk = chunks(x_hbm, x_ref, sems, 3)
    for k in range(TOK // 8):
        chunk(k).start()
    for copy in loads:
        copy.wait()
    st = st_ref[...]
    w2 = jnp.concatenate(split2(dot_nt(st, w_ref[...])), axis=0)
    e_hi, e_low = split2(e_ref[...])
    eh_ref[...] = e_hi
    es = dot_nt(st, e_hi) + dot_nt(st, e_low)
    es4 = jnp.concatenate([es] * GROUP, axis=1)
    core = lax.axis_index("core")

    wide = 4

    @pl.loop(0, TOK // 8 // wide)
    def _(it):
        for k in range(wide):
            chunk(it * wide + k).wait()
        spots = [pl.multiple_of((it * wide * 2 + k) * block, block) for k in range(2 * wide)]
        xs = [x_ref[pl.ds(at, block), :] for at in spots]
        twos = [dot_nt(w2, xg) for xg in xs]
        ss = [s2[:HEADS] + s2[HEADS:] + es4 for s2 in twos]
        for at, s in zip(spots, ss):
            score_ref[:, pl.ds(at, block)] = s
        mask = same_token()
        sx = [jnp.where(mask, jnp.concatenate([s] * GROUP, axis=0), -jnp.inf) for s in ss]
        tops = [jnp.max(s, axis=1, keepdims=True) for s in sx]
        ws = [jnp.exp(s - m) for s, m in zip(sx, tops)]
        totals = [jnp.sum(w, axis=1, keepdims=True) for w in ws]
        ws = [w * (1.0 / total) for w, total in zip(ws, totals)]
        ys = [dot(w.astype(BF16), xg) for w, xg in zip(ws, xs)]
        cols = [m + jnp.log(total) for m, total in zip(tops, totals)]
        for k, (y, w) in enumerate(zip(ys, ws)):
            rows = GROUP * HEADS
            rows = pl.ds(pl.multiple_of((it * wide * 2 + k) * rows, rows), rows)
            y_ref[rows, :] = y.astype(BF16)
            p_ref[rows, :] = fold(w).astype(BF16)
        size = 8 * wide
        lane_ref[pl.ds(pl.multiple_of(it * size, size), size), :] = as_lanes(
            jnp.concatenate(cols, axis=0), size
        )

    @pl.loop(0, TOK // 16, unroll=2)
    def _(it):
        rows = pl.ds(pl.multiple_of(it * 16 * HEADS, 16 * HEADS), 16 * HEADS)
        out = dot(y_ref[rows, :], w_ref[...]) + dot(p_ref[rows, :], eh_ref[...])
        out = jnp.where(head_select(16), out.reshape(16, HEADS, D), 0.0)
        out = jnp.sum(out, axis=1)
        parts = lane_ref[pl.ds(pl.multiple_of(it * 16, 16), 16), :]
        first = core == 0
        to = pl.ds(pl.multiple_of(it * 8, 8), 8)
        keep_ref[to, :D] = jnp.where(first, out[:8], out[8:]).astype(BF16)
        send_ref[to, :D] = jnp.where(first, out[8:], out[:8]).astype(BF16)
        keep_ref[to, D:] = pack_parts(jnp.where(first, parts[:8], parts[8:]))
        send_ref[to, D:] = pack_parts(jnp.where(first, parts[8:], parts[:8]))


def merge(outs, parts):
    rows = outs[0].shape[0]
    lses = [unpack_parts(p) for p in parts]
    top = functools.reduce(jnp.maximum, lses)
    es = [jnp.exp(v - top) for v in lses]
    total = sum(es)
    weight = jnp.concatenate([e / total for e in es], axis=0)
    hi, low = split2(weight)
    spread = head_spread()
    wide = dot(hi, spread) + dot(low, spread)
    out = sum(o.astype(F32) * wide[k * rows : (k + 1) * rows] for k, o in enumerate(outs))
    return out, top + jnp.log(total)


def pair_kernel(keep_ref, got_ref, cot_ref, pay_ref):
    out, lse = merge([keep_ref[:, :D], got_ref[:, :D]], [keep_ref[:, D:], got_ref[:, D:]])
    pay_ref[:HALF, :D] = out.astype(BF16)
    pay_ref[:HALF, D:] = pack_parts(lse)
    pay_ref[HALF:, :D] = cot_ref[...]
    pay_ref[HALF:, D:] = jnp.zeros((8, 128), BF16)


def combine_kernel(p0_ref, p1_ref, p2_ref, p3_ref, ow_ref, gain_ref, pay_ref, mix_ref):
    refs = (p0_ref, p1_ref, p2_ref, p3_ref)
    out, lse = merge([r[:HALF, :D] for r in refs], [r[:HALF, D:] for r in refs])
    agg = out.astype(BF16)
    mix = dot(agg, ow_ref[...])
    scale = lax.rsqrt(jnp.mean(mix * mix, axis=1, keepdims=True) + EPSILON)
    pay_ref[:, :D] = (mix * scale * gain_ref[...]).astype(BF16)
    pay_ref[:, D:PAY] = pack_parts(lse)
    x = lax.axis_index("x")
    for k in range(NX):
        rows = pl.ds(pl.multiple_of(lax.rem(x + (NX - k), NX) * 8, 8), 8)
        pay_ref[rows, PAY:] = refs[k][HALF:, :D]
    mix_ref[0] = mix
    mix_ref[1] = agg.astype(F32)


def tokens(a_ref, b_ref, start, stop):
    return jnp.concatenate([a_ref[:, start:stop], b_ref[:, start:stop]], axis=0)


def mlp_kernel(a_ref, b_ref, up_ref, down_ref, act_ref, gpre_ref, keep_ref, send_ref):
    normed = tokens(a_ref, b_ref, 0, D)
    cot = tokens(a_ref, b_ref, PAY, PAY + D)
    x = dot(normed, up_ref[...])
    c = np.float32(np.sqrt(2 / np.pi))
    t = jnp.tanh(c * (x + 0.044715 * (x * x * x)))
    act_ref[...] = (0.5 * x * (1.0 + t)).astype(BF16)
    slope = 0.5 * (1.0 + t) + 0.5 * x * (1.0 - t * t) * (c * (1.0 + (3 * 0.044715) * (x * x)))
    gpre = (dot_nt(cot, down_ref[...]) * slope).astype(BF16)
    gpre_ref[...] = gpre
    gn = dot_nt(gpre, up_ref[...]).astype(BF16)
    keep_ref[...] = gn[:HALF]
    send_ref[...] = gn[HALF:]


def mlp_out_kernel(a_ref, b_ref, act_ref, gpre_ref, down_ref, keep_ref, send_ref, ypay_ref):
    act = act_ref[...]
    out = dot(act, down_ref[...]).astype(BF16)
    keep_ref[...] = out[:HALF]
    send_ref[...] = out[HALF:]
    source, target = iota((FFL, FFL), 0), iota((FFL, FFL), 1)
    to, rest = target >> 6, target & 63
    perm = (source == ((rest >> 4) << 7) + (to << 4) + (rest & 15)).astype(F32).astype(BF16)
    act_y = dot(act, perm).astype(BF16)
    source, target = iota((D, D), 0), iota((D, D), 1)
    to, rest = target >> 7, target & 127
    perm = (source == ((rest >> 5) << 8) + (to << 5) + (rest & 31)).astype(F32).astype(BF16)
    norm_y = dot(tokens(a_ref, b_ref, 0, D), perm).astype(BF16)
    cot = tokens(a_ref, b_ref, PAY, PAY + D)
    gpre = gpre_ref[...]
    pad = jnp.zeros((TOK, 64), BF16)
    for k in range(NNEAR):
        ypay_ref[k, :, :FFL] = gpre
        ypay_ref[k, :, FFL : FFL + 128] = norm_y[:, 128 * k : 128 * (k + 1)]
        ypay_ref[k, :, FFL + 128 : FFL + 128 + D] = cot
        ypay_ref[k, :, FFL + 128 + D :] = jnp.concatenate([act_y[:, 64 * k : 64 * (k + 1)], pad], axis=1)


def weight_kernel(in_ref, out_ref):
    rows = NNEAR * TOK
    gpre = in_ref[:, :, :FFL].reshape(rows, FFL)
    normed = in_ref[:, :, FFL : FFL + 128].reshape(rows, 128)
    cot = in_ref[:, :, FFL + 128 : FFL + 128 + D].reshape(rows, D)
    act = in_ref[:, :, FFL + 128 + D :].reshape(rows, 128)
    up = dot_tn(normed, gpre).astype(BF16)
    down = dot_tn(act, cot)[:64].astype(BF16)
    for k in range(FFL // 128):
        cols, more = slice(128 * k, 128 * (k + 1)), slice(FFL + 128 * k, FFL + 128 * (k + 1))
        out_ref[:, 64 * k : 64 * k + 32, :] = up[:, cols].reshape(NFAR, 32, 128)
        out_ref[:, 64 * k + 32 : 64 * k + 48, :] = down[:, cols].reshape(NFAR, 16, 128)
        out_ref[:, 64 * k + 48 : 64 * k + 64, :] = down[:, more].reshape(NFAR, 16, 128)


def add_kernel(a_ref, b_ref, _, out_ref):
    out_ref[...] = (a_ref[...].astype(F32) + b_ref[...].astype(F32)).astype(BF16)


def mix_grad_kernel(
    g0_ref, g1_ref, g2_ref, g3_ref, mix_ref, n_ref, ow_hbm, gain_ref, pay_ref, ow_ref, sem
):
    load = pltpu.make_async_copy(ow_hbm, ow_ref, sem)
    load.start()
    gn = sum(r[...].astype(F32) for r in (g0_ref, g1_ref, g2_ref, g3_ref))
    mix = mix_ref[0]
    scale = lax.rsqrt(jnp.mean(mix * mix, axis=1, keepdims=True) + EPSILON)
    g = gn * gain_ref[...]
    pull = g * scale - mix * (scale * scale * scale * jnp.mean(mix * g, axis=1, keepdims=True))
    half = (n_ref[:, PAY:].astype(F32) + pull).astype(BF16)
    load.wait()
    ga = dot_nt(half, ow_ref[...]).astype(BF16)
    hi, mid, low = split3(ga.astype(F32) * mix_ref[1])
    spread = head_spread()
    dots = dot_nt(hi, spread) + dot_nt(mid, spread) + dot_nt(low, spread)
    pay_ref[:, :D] = ga
    pay_ref[:, D:] = pack_parts(dots)


def backward_kernel(
    x_ref, w_ref, st_ref, eh_ref, score_ref, na_ref, nb_ref, ga_ref, gb_ref, keep_ref, send_ref, chan_ref,
    left_ref, right_ref, back_ref, be_ref, z_ref, sg_ref,
):
    st = st_ref[...]
    block = GROUP * CH
    z_ref[...] = jnp.zeros_like(z_ref)
    sg_ref[...] = jnp.zeros_like(sg_ref)
    core = lax.axis_index("core")
    first = core == 0

    @pl.loop(0, TOK // 16)
    def _(it):
        at = pl.ds(pl.multiple_of(it * 8, 8), 8)
        mine, other = ga_ref[at, :D].astype(F32), gb_ref[at, :D].astype(F32)
        ga = jnp.concatenate([jnp.where(first, mine, other), jnp.where(first, other, mine)], axis=0)
        gx = jnp.where(head_select(16), jnp.broadcast_to(ga[:, None, :], (16, HEADS, D)), 0.0)
        gx = gx.reshape(16 * HEADS, D).astype(BF16)
        rows = pl.ds(pl.multiple_of(it * 16 * HEADS, 16 * HEADS), 16 * HEADS)
        right_ref[rows, :] = gx
        back_ref[rows, :] = dot_nt(gx, w_ref[...]).astype(BF16)
        be = dot_nt(gx, eh_ref[...])
        be_ref[rows, :] = jnp.concatenate([be] * GROUP, axis=1)

    wide = 2

    @pl.loop(0, TOK // 8 // wide)
    def _(it):
        size = GROUP * HEADS
        lses, dots = [], []
        for k in range(wide):
            octet = it * wide + k
            rows = pl.ds(pl.multiple_of((octet // 2) * 8, 8), 8)
            mine = octet % 2 == core
            lse = jnp.where(mine, na_ref[rows, D:PAY].astype(F32), nb_ref[rows, D:PAY].astype(F32))
            lse = as_column(unpack_parts(lse), 8)
            dot_ = jnp.where(mine, ga_ref[rows, D:].astype(F32), gb_ref[rows, D:].astype(F32))
            dot_ = as_column(unpack_parts(dot_), 8)
            lses += [lse[:size], lse[size:]]
            dots += [dot_[:size], dot_[size:]]
        spots = [pl.multiple_of((it * wide * 2 + k) * block, block) for k in range(2 * wide)]
        bases = [pl.ds(pl.multiple_of((it * wide * 2 + k) * size, size), size) for k in range(2 * wide)]
        xs = [x_ref[pl.ds(at, block), :] for at in spots]
        heads = [dot_nt(back_ref[base, :], xg) + be_ref[base, :] for base, xg in zip(bases, xs)]
        ss = [score_ref[:, pl.ds(at, block)] for at in spots]
        mask = same_token()
        sx = [
            jnp.where(mask, jnp.concatenate([s] * GROUP, axis=0) - lse, -jnp.inf)
            for s, lse in zip(ss, lses)
        ]
        ps = [jnp.exp(s) for s in sx]
        sgs = [p * (head - d) for p, head, d in zip(ps, heads, dots)]
        sgs = [jnp.sum(sg.reshape(GROUP, HEADS, block), axis=0) for sg in sgs]
        yzs = [
            dot(jnp.concatenate([p, sg], axis=0).astype(BF16), xg) for p, sg, xg in zip(ps, sgs, xs)
        ]
        for base, yz, p in zip(bases, yzs, ps):
            left_ref[base, :PIX] = yz[:size].astype(BF16)
            pc = fold(p)
            left_ref[base, PIX:] = jnp.concatenate([pc, pc], axis=1).astype(BF16)
        z_ref[...] += sum(yz[size:] for yz in yzs)
        sg_ref[...] += sum(sgs)

    sg = sg_ref[...]
    sgc = fold(sg)
    last = jnp.concatenate([z_ref[...], sgc, sgc], axis=1)
    tail_hi, tail_low = split2(last)
    out = dot_tn(left_ref[...], right_ref[...]) + dot_tn(tail_hi, st) + dot_tn(tail_low, st)
    for k in range(NX):
        even = out[:PIX, 256 * k : 256 * k + 128]
        odd = out[:PIX, 256 * k + 128 : 256 * (k + 1)]
        keep_ref[k] = jnp.where(core == 0, even, odd).astype(BF16)
        send_ref[k] = jnp.where(core == 0, odd, even).astype(BF16)
    for k in range(NCHAN):
        piece = out[PIX : PIX + CH, 128 * k : 128 * (k + 1)]
        chan_ref[:, 2 * k : 2 * k + 2, :] = piece.reshape(NSPACE, 2, 128).astype(BF16)


def patch_pair_kernel(keep_ref, got_ref, okeep_ref, ogot_ref, *out_refs):
    x = lax.axis_index("x")
    for o, out_ref in enumerate(out_refs):
        to = lax.rem(x + o, NX)
        out_ref[:PIX, :] = (keep_ref[to].astype(F32) + got_ref[to].astype(F32)).astype(BF16)
        rows = pl.ds(pl.multiple_of(to * 8, 8), 8)
        both = okeep_ref[rows, :].astype(F32) + ogot_ref[rows, :].astype(F32)
        for k in range(8):
            out_ref[PIX + 8 * k : PIX + 8 * (k + 1), :] = both[:, 128 * k : 128 * (k + 1)].astype(BF16)


def patch_sum_kernel(p0_ref, p1_ref, p2_ref, p3_ref, chan_ref, mix_ref, _, out_ref, pay_ref):
    total = sum(r[...].astype(F32) for r in (p0_ref, p1_ref, p2_ref, p3_ref))
    patch = total[:PIX].astype(BF16).reshape(NFAR, NNEAR, 8, 128)
    chan = chan_ref[...].reshape(NFAR, NNEAR, 16, 128)
    for k in range(NFAR):
        pay_ref[:, k, :8, :] = patch[k]
        pay_ref[:, k, 8:, :] = chan[k]
    x = lax.axis_index("x")
    mix = mix_ref[0, pl.ds(pl.multiple_of(x * 8, 8), 8), :]
    for k in range(8):
        cols = slice(128 * k, 128 * (k + 1))
        out_ref[:, cols] = (mix[:, cols] + total[PIX + 8 * k : PIX + 8 * (k + 1)]).astype(BF16)


def strip_sum_kernel(in_ref, z_ref, out_ref):
    out_ref[:, :256, :] = z_ref[...]
    out_ref[:, 256:, :] = jnp.sum(in_ref[...].astype(F32), axis=0).astype(BF16)


def last_kernel(in_ref, patch_ref, chan_ref, up_ref, down_ref):
    total = jnp.sum(in_ref[...].astype(F32), axis=0)
    for k in range(FFL // 128):
        cols, more = slice(128 * k, 128 * (k + 1)), slice(FFL + 128 * k, FFL + 128 * (k + 1))
        up_ref[:, cols] = total[64 * k : 64 * k + 32]
        down_ref[:, cols] = total[64 * k + 32 : 64 * k + 48]
        down_ref[:, more] = total[64 * k + 48 : 64 * k + 64]
    patch_ref[...] = total[256:264]
    for k in range(8):
        chan_ref[:, 128 * k : 128 * (k + 1)] = total[264 + 2 * k : 266 + 2 * k]


def call(kernel, outs, args, scratch=(), flops=0, nbytes=0, limit=16, hbm=()):
    spaces = [pltpu.HBM if k in hbm else pltpu.VMEM for k in range(len(args))]
    return pl.pallas_call(
        kernel,
        out_shape=[jax.ShapeDtypeStruct(s, d) for s, d in outs],
        in_specs=[pl.BlockSpec(memory_space=space) for space in spaces],
        scratch_shapes=list(scratch),
        cost_estimate=pl.CostEstimate(flops=flops, bytes_accessed=nbytes, transcendentals=0),
        compiler_params=pltpu.CompilerParams(vmem_limit_bytes=limit << 20),
    )(*(pltpu.with_memory_space_constraint(a, pltpu.HBM) if k in hbm else a for k, a in enumerate(args)))


def exchange(x, axes):
    return lax.all_to_all(x, axes, 0, 0, tiled=True)


def swap(x):
    return lax.ppermute(x, "core", [(0, 1), (1, 0)])


def shift(x, o, axis="x", size=NX):
    return lax.ppermute(x, axis, [(i, (i + o) % size) for i in range(size)])


def around(x):
    return [x] + [shift(x, o) for o in range(1, NX)]


def forward(x, patch_weight, st, channel_embed):
    return call(
        forward_kernel,
        [
            ((HEADS, TOK * CH), F32), ((HALF, PAY), BF16), ((HALF, PAY), BF16),
            ((PIX, D), BF16), ((HEADS, D), BF16), ((CH, D), BF16),
        ],
        (x, patch_weight, st, channel_embed),
        [
            pltpu.VMEM((TOK * CH, PIX), BF16),
            pltpu.VMEM((CH, D), F32),
            pltpu.VMEM((TOK * HEADS, PIX), BF16),
            pltpu.VMEM((TOK * HEADS, CH), BF16),
            pltpu.VMEM((TOK, 128), F32),
            pltpu.SemaphoreType.DMA((3 + TOK // 8,)),
        ],
        flops=4 << 30, nbytes=4 << 20, limit=24, hbm=(0, 1, 2, 3),
    )


def backward(x, w, st, eh, score, npay, nother, gpay, gother):
    return call(
        backward_kernel,
        [((NX, PIX, 128), BF16), ((NX, PIX, 128), BF16), ((NSPACE, 16, 128), BF16)],
        (x, w, st, eh, score, npay, nother, gpay, gother),
        [
            pltpu.VMEM((TOK * HEADS, PIX + 128), BF16),
            pltpu.VMEM((TOK * HEADS, D), BF16),
            pltpu.VMEM((TOK * HEADS, PIX), BF16),
            pltpu.VMEM((TOK * HEADS, PIX), F32),
            pltpu.VMEM((HEADS, PIX), F32),
            pltpu.VMEM((HEADS, GROUP * CH), F32),
        ],
        flops=52 << 29, nbytes=1 << 20, limit=24,
    )


def on_device(
    patches, patch_weight, channel_embed, score_map, out_weight, norm_gain, up_weight, down_weight, cotangent
):
    gain = norm_gain.reshape(1, D)
    x = patches.reshape(TOK * CH, PIX)
    score, keep, send, w, st, eh = forward(x, patch_weight, score_map.T, channel_embed)
    (pay,) = call(
        pair_kernel, [((HALF + 8, PAY), BF16)], (keep, swap(send), cotangent[0]),
        flops=1 << 29, nbytes=1 << 18,
    )
    npay, mix = call(
        combine_kernel,
        [((HALF, PAY + D), BF16), ((2, HALF, D), F32)],
        (*around(pay), out_weight, gain),
        flops=1 << 30, nbytes=3 << 20,
    )
    nother = swap(npay)
    act, gpre, gkeep, gsend = call(
        mlp_kernel,
        [((TOK, FFL), BF16), ((TOK, FFL), BF16), ((HALF, D), BF16), ((HALF, D), BF16)],
        (npay, nother, up_weight, down_weight),
        flops=1 << 30, nbytes=3 << 20,
    )
    okeep, osend, ypay = call(
        mlp_out_kernel,
        [((HALF, D), BF16), ((HALF, D), BF16), ((NNEAR, TOK, YPAY), BF16)],
        (npay, nother, act, gpre, down_weight),
        flops=1 << 30, nbytes=3 << 20,
    )
    (gsum,) = call(
        add_kernel, [((HALF, D), BF16)], (gkeep, swap(gsend), okeep), flops=1 << 20, nbytes=1 << 18
    )
    ogot = swap(osend)
    yfull = exchange(ypay, NEAR)
    (gpay,) = call(
        mix_grad_kernel, [((HALF, PAY), BF16)],
        (*around(gsum), mix, npay, out_weight, gain),
        flops=4 << 29, nbytes=3 << 20, hbm=(6,),
        scratch=[pltpu.VMEM((D, D), BF16), pltpu.SemaphoreType.DMA],
    )
    gother = swap(gpay)
    pkeep, psend, chan = backward(x, w, st, eh, score, npay, nother, gpay, gother)
    own, *away = call(
        patch_pair_kernel, [((PIX + 64, 128), BF16)] * NX, (pkeep, swap(psend), okeep, ogot),
        flops=1 << 20, nbytes=1 << 20,
    )
    (zpay,) = call(
        weight_kernel, [((NFAR, 256, 128), BF16)], (yfull,), flops=1 << 28, nbytes=3 << 20
    )
    layer_out, strip = call(
        patch_sum_kernel,
        [((8, D), BF16), ((NNEAR, NFAR, 24, 128), BF16)],
        (own, *[shift(v, o) for o, v in enumerate(away, 1)], chan, mix, zpay),
        flops=1 << 20, nbytes=1 << 20,
    )
    (spay,) = call(
        strip_sum_kernel, [((NFAR, 280, 128), BF16)], (exchange(strip, NEAR), zpay),
        flops=1 << 20, nbytes=1 << 20,
    )
    patch_grad, channel_grad, up_grad, down_grad = call(
        last_kernel,
        [((8, 128), F32), ((2, D), F32), ((32, FFL), F32), ((16, D), F32)],
        (exchange(spay, ("far",)),),
        flops=1 << 20, nbytes=1 << 20,
    )
    return layer_out[None], up_grad, down_grad, patch_grad, channel_grad


def solution(mesh):
    fine = Mesh(np.asarray(mesh.devices).reshape(4, 2, NFAR, 2, 4), ("x", "core", "far", "low", "y"))
    return jax.shard_map(
        on_device,
        mesh=fine,
        in_specs=(
            P(SPACE, None, CHAN, None),
            P(),
            P(CHAN, None),
            P(),
            P(),
            P(),
            P(None, CHAN),
            P(CHAN, None),
            P(SPACE, CHAN, None),
        ),
        out_specs=(
            P(SPACE, CHAN, None),
            P(SPACE, CHAN),
            P((*CHAN, *SPACE), None),
            P(SPACE, CHAN),
            P((*CHAN, *SPACE), None),
        ),
        check_vma=False,
    )
```
